32 devices in a mesh: edge: 4 (over y, x), tile: 8 (over z, core).
Axes of the slice: x: 2, y: 2, z: 4, core: 2. Of those that a mesh axis runs over, the one named last changes fastest.
Arguments:
- features: bfloat16 [96, 48, 64, 128], P('edge', 'tile'), may hold values from -6 to 6
- hidden_state: bfloat16 [32, 48, 64, 128], P('edge', 'tile'), may hold values from -1 to 1
- edge_source: int32 [32], P('edge'), may hold values from 0 to 23
- edge_owner: int32 [32, 1], P('edge'), may hold values from 0 to 3; in each aligned block of 8 rows (0 to 7, 8 to 15, ...) at most 4 rows name the same one
- edge_target: int32 [32], P('edge'), may hold values from 0 to 23
- edge_counts: int32 [4], P('edge'), may hold values from 4 to 8, as said below
- corr_weight: bfloat16 [49, 128], replicated, may hold values from -0.875 to 0.875
- gate_weight: bfloat16 [3, 3, 256, 256], replicated, may hold values from -0.125 to 0.125
- candidate_weight: bfloat16 [3, 3, 256, 128], replicated, may hold values from -0.125 to 0.125
- jacobian_weight: bfloat16 [128, 24], replicated, may hold values from -0.5 to 0.5
- confidence_weight: bfloat16 [128, 2], replicated, may hold values from -3 to 3
Outputs:
- hidden_next: bfloat16 [32, 48, 64, 128], P('edge', 'tile')
- camera_hessian: float32 [576, 576], P('tile', 'edge')
- pose_diagonal: float32 [96, 36], P('edge')
The draws below stay inside these ranges and needn't reach their ends.
Inputs may be any that keep to these rules, and one draw needn't show every extreme that they name: `edge_owner`: in the rows of one index of edge at most 4 edges name the same owner, a bound that some block reaches. `edge_counts`: edges past a device's count are unused; some index of edge uses all 8.
All inputs are finite; a program needn't handle non-finite values.
Results may differ from the reference program's by a relative error of at most 0.015.
Values may be sent and summed in bfloat16 or wider, within the bound.
A program may use at most 128 MiB of HBM per device.

```python
import math
import jax
import jax.numpy as jnp
import numpy as np
from jax import lax

MAPH = 48
MAPW = 64
CH = 128
HID = 128
WINDOW = 7
FRAMES_DEV = 24
EDGES_DEV = 8
MOST = 4
FRAMES = 96
EDGES = 32
N_EDGE = 4


def draw_edge_counts(key, part):
    devices = EDGES // EDGES_DEV
    first_key, second_key = jax.random.split(jax.random.fold_in(key, 17))
    counts = jax.random.randint(first_key, (devices,), EDGES_DEV // 2, EDGES_DEV + 1)
    fullest = jax.random.randint(second_key, (), 0, devices)
    return jnp.where(jnp.arange(devices) == fullest, EDGES_DEV, counts).astype(jnp.int32)


def plant(entries, key, least, top_value):
    spot = [jax.random.randint(jax.random.fold_in(key, axis), (), 0, length) for axis, length in enumerate(entries.shape)]
    main_axis = entries.shape.index(max(entries.shape))
    beside = spot[:main_axis] + [(spot[main_axis] + 1) % entries.shape[main_axis]] + spot[main_axis + 1:]
    return entries.at[tuple(spot)].set(least).at[tuple(beside)].set(top_value)


def block_levels(rng, extent, shards, low, top_value):
    factor_of = 1.0
    for position, shards_of in shards:
        draws = jax.random.uniform(jax.random.fold_in(jax.random.fold_in(rng, 6), position), (shards_of,), jnp.float32, low / len(shards), top_value / len(shards))
        factor_of = factor_of * jnp.repeat(jnp.exp(draws), extent[position] // shards_of).reshape((-1,) + (1,) * (len(extent) - 1 - position))
    return factor_of


def routed_block(rng, own, number, rows, amount, top, reach, lean):
    ranking = jax.random.permutation(rng, amount)
    crowded, usual = shares(amount, rows * top, reach, lean, True), shares(amount, rows * top, reach, lean, False)
    places = jnp.arange(amount)

    def named(lengths, rotation):
        used = int((lengths > 0).sum())
        fixed = max(1, used // 4)
        passed = fixed + (places - fixed + rotation * (used - fixed)) % max(1, amount - fixed)
        return jnp.zeros((amount,), jnp.int32).at[ranking[jnp.where(places < fixed, places, passed)]].set(jnp.asarray(lengths, jnp.int32))

    lengths = jnp.where(number % 4 == 0, named(crowded, number // 4), named(usual, number - number // 4 - 1))
    mixed = jax.random.permutation(jax.random.fold_in(own, 3), amount)
    source_of, taker = mixed[0:amount // 2 * 2:2], mixed[1:amount // 2 * 2:2]
    margin = jnp.minimum(lengths[source_of] - 1, reach - lengths[taker]) // 2
    margin = jnp.where((source_of == ranking[0]) | (taker == ranking[0]) | (lengths[taker] == 0), 0, jnp.maximum(margin, 0))
    passed = jax.random.randint(jax.random.fold_in(own, 4), (amount // 2,), 0, 1 << 20) % (margin + 1)
    lengths = lengths.at[source_of].add(-passed).at[taker].add(passed)
    labels = jnp.searchsorted(jnp.cumsum(lengths), jnp.arange(rows * top), side="right").astype(jnp.int32)
    table = labels.reshape(top, rows).T
    table = table[jax.random.permutation(jax.random.fold_in(own, 1), rows)]
    rotation = jax.random.randint(jax.random.fold_in(own, 2), (rows, 1), 0, top)
    return jnp.take_along_axis(table, (jnp.arange(top)[None, :] + rotation) % top, axis=1)


def shares(count, total, bound, slope, full):
    loads = [(1 << 20) // math.isqrt(standing ** slope) + 1 for standing in range(1, count + 1)]
    largest = bound if full else min(bound, max(-(-total // count), total * loads[0] // sum(loads)))
    least = 1 if total - largest >= count - 1 else 0
    holding, surplus = [largest] + [least] * (count - 1), total - largest - least * (count - 1)
    while surplus > 0:
        candidates = [i for i in range(1, count) if holding[i] < largest] or [i for i in range(1, count) if holding[i] < bound]
        whole, left = sum([loads[i] for i in candidates]), surplus
        for i in candidates:
            more = min(bound - holding[i], max(1, left * loads[i] // whole), surplus)
            holding[i] = holding[i] + more
            surplus = surplus - more
    return np.array(holding)


def noise(own_key, dims, spread, most, shards=(), kind=jnp.bfloat16):
    loudness = block_levels(own_key, dims, shards, -0.22, 0.18) if shards else 1.0
    array = jax.random.normal(own_key, dims, jnp.float32) * spread * loudness
    return jnp.minimum(jnp.maximum(array, -most), most).astype(kind)


def setup_inputs(seed: int = 0) -> dict:
    seeds = jax.random.split(jax.random.key(seed), 12)
    features = noise(seeds[0], (FRAMES, MAPH, MAPW, CH), 1.0, 6.0, ((0, 4), (1, 8)))
    hidden_state = jnp.clip(jax.random.uniform(seeds[1], (EDGES, MAPH, MAPW, HID), jnp.float32, -1.0, 1.0) * block_levels(seeds[1], (EDGES, MAPH, MAPW, HID), ((0, 4), (1, 8)), -0.4, 0.0), -1.0, 1.0).astype(jnp.bfloat16)
    edge_source = plant(jax.random.randint(seeds[2], (EDGES,), 0, FRAMES_DEV), jax.random.fold_in(seeds[2], 1), 0, FRAMES_DEV - 1).astype(jnp.int32)
    edge_owner_keys = jax.random.split(jax.random.fold_in(seeds[3], 1), EDGES // EDGES_DEV)
    edge_owner_turns = jax.random.permutation(jax.random.fold_in(seeds[3], 3), EDGES // EDGES_DEV)
    edge_owner = jax.vmap(lambda own, number: routed_block(jax.random.fold_in(seeds[3], 2), own, number, EDGES_DEV, N_EDGE, 1, MOST, 1))(edge_owner_keys, edge_owner_turns).reshape((EDGES, 1))
    edge_target = plant(jax.random.randint(seeds[4], (EDGES,), 0, FRAMES_DEV), jax.random.fold_in(seeds[4], 1), 0, FRAMES_DEV - 1).astype(jnp.int32)
    edge_counts = draw_edge_counts(jax.random.fold_in(seeds[11], 71), 0)
    corr_weight = noise(seeds[6], (WINDOW * WINDOW, HID), (WINDOW * WINDOW) ** -0.5, 0.875)
    gate_weight = noise(seeds[7], (3, 3, 2 * HID, 2 * HID), (18 * HID) ** -0.5, 0.125)
    candidate_weight = noise(seeds[8], (3, 3, 2 * HID, HID), (18 * HID) ** -0.5, 0.125)
    jacobian_weight = noise(seeds[9], (HID, 24), HID ** -0.5, 0.5)
    confidence_weight = noise(seeds[10], (HID, 2), 0.5, 3.0)
    return dict(features=features, hidden_state=hidden_state, edge_source=edge_source, edge_owner=edge_owner, edge_target=edge_target, edge_counts=edge_counts, corr_weight=corr_weight, gate_weight=gate_weight, candidate_weight=candidate_weight, jacobian_weight=jacobian_weight, confidence_weight=confidence_weight)


def convolve(padded, weight):
    row_count = padded.shape[0] - 2
    col_count = padded.shape[1] - 2
    running = jnp.zeros((row_count, col_count, weight.shape[-1]), jnp.float32)
    for row_step in range(3):
        for col_step in range(3):
            window = padded[row_step:row_step + row_count, col_step:col_step + col_count].astype(jnp.float32)
            running = running + jnp.einsum('rwc,ck->rwk', window, weight[row_step, col_step].astype(jnp.float32))
    return running


def pad_map(values):
    return jnp.pad(values, ((1, 1), (1, 1), (0, 0)))


def window_corr(source_map, target_map):
    radius = WINDOW // 2
    padded = jnp.pad(target_map, ((radius, radius), (radius, radius), (0, 0)))
    columns = []
    for row_shift in range(WINDOW):
        for col_shift in range(WINDOW):
            moved = padded[row_shift:row_shift + MAPH, col_shift:col_shift + MAPW]
            columns.append(jnp.sum(source_map * moved, axis=-1))
    return jnp.stack(columns, axis=-1) * (CH ** -0.5)


def reference(features, hidden_state, edge_source, edge_owner, edge_target, edge_counts, corr_weight, gate_weight, candidate_weight, jacobian_weight, confidence_weight):
    edge_index = jnp.arange(EDGES, dtype=jnp.int32)
    device_of = edge_index // EDGES_DEV
    in_use = ((edge_index % EDGES_DEV) < edge_counts[device_of]).astype(jnp.float32)
    source_global = (device_of * FRAMES_DEV + edge_source).astype(jnp.int32)
    target_global = (edge_owner[:, 0] * FRAMES_DEV + edge_target).astype(jnp.int32)

    def edge_update(inputs):
        source_frame, target_frame, state, usage = inputs
        source_map = features[source_frame].astype(jnp.float32)
        target_map = features[target_frame].astype(jnp.float32)
        corr = window_corr(source_map, target_map).astype(jnp.bfloat16)
        motion = jax.nn.relu(jnp.einsum('rcd,dk->rck', corr.astype(jnp.float32), corr_weight.astype(jnp.float32))).astype(jnp.bfloat16)
        stacked = jnp.concatenate([state, motion], axis=-1)
        gates = jax.nn.sigmoid(convolve(pad_map(stacked), gate_weight))
        update = gates[..., :HID]
        reset = gates[..., HID:]
        state_float = state.astype(jnp.float32)
        reset_state = (reset * state_float).astype(jnp.bfloat16)
        mixed = jnp.concatenate([reset_state, motion], axis=-1)
        candidate = jnp.tanh(convolve(pad_map(mixed), candidate_weight))
        new_state = ((1.0 - update) * state_float + update * candidate).astype(jnp.bfloat16)
        new_float = new_state.astype(jnp.float32)
        jacobian = jnp.einsum('rwh,hk->krw', new_float, jacobian_weight.astype(jnp.float32)).reshape(2, 12, MAPH * MAPW)
        confidence = jax.nn.softplus(jnp.einsum('rwh,hk->krw', new_float, confidence_weight.astype(jnp.float32))).reshape(2, 1, MAPH * MAPW)
        normal_block = jnp.einsum('kap,kbp->ab', jacobian * confidence, jacobian, precision=lax.Precision.HIGHEST) / (MAPH * MAPW)
        normal_block = normal_block * usage
        kept = jnp.where(usage > 0, new_state, state)
        return kept, normal_block

    hidden_next, normal_blocks = lax.map(edge_update, (source_global, target_global, hidden_state, in_use))
    blocks4 = jnp.zeros((FRAMES, FRAMES, 6, 6), jnp.float32)
    blocks4 = blocks4.at[source_global, source_global].add(normal_blocks[:, :6, :6])
    blocks4 = blocks4.at[source_global, target_global].add(normal_blocks[:, :6, 6:])
    blocks4 = blocks4.at[target_global, source_global].add(normal_blocks[:, 6:, :6])
    blocks4 = blocks4.at[target_global, target_global].add(normal_blocks[:, 6:, 6:])
    frame_index = jnp.arange(FRAMES, dtype=jnp.int32)
    pose_diagonal = blocks4[frame_index, frame_index].reshape(FRAMES, 36)
    blocks4 = blocks4.at[frame_index, frame_index].set(jnp.zeros((FRAMES, 6, 6), jnp.float32))
    camera_hessian = blocks4.transpose(0, 2, 1, 3).reshape(6 * FRAMES, 6 * FRAMES)
    return hidden_next, camera_hessian, pose_diagonal
```

```python
import functools

import jax
import jax.numpy as jnp
from jax import lax
from jax.experimental import pallas as pl
from jax.experimental.pallas import tpu as pltpu
from jax.sharding import PartitionSpec as P

MAPH = 48
WINDOW = 7
RADIUS = WINDOW // 2
MESH = pl.DeviceIdType.MESH
HIGH = lax.Precision.HIGHEST
BF = jnp.bfloat16
F32 = jnp.float32


def nt(a, b, precision=None):
    return lax.dot_general(
        a, b, (((1,), (1,)), ((), ())), preferred_element_type=F32, precision=precision
    )


def nn(a, b, precision=None):
    return lax.dot_general(
        a, b, (((1,), (0,)), ((), ())), preferred_element_type=F32, precision=precision
    )


def iota(shape, dim):
    return lax.broadcasted_iota(jnp.int32, shape, dim)


def sixth(index):
    return jnp.floor((index.astype(F32) + 0.5) * (1.0 / 6.0))


def kernel(
    dims,
    meta_in,
    feat,
    hidden,
    corr_w,
    gate_w,
    cand_w,
    head_w,
    out_hidden,
    out_cam,
    out_diag,
    meta_all,
    meta_s,
    send,
    text,
    sref,
    hext,
    mext,
    rext,
    x3,
    wh,
    wm,
    wr,
    gpre,
    cpre,
    upd,
    gpart,
    gtile,
    gsum,
    gall,
    s_meta,
    r_meta,
    l_meta,
    s_feat,
    r_feat,
    s_tup,
    r_tup,
    s_tdn,
    r_tdn,
    s_hup,
    r_hup,
    s_hdn,
    r_hdn,
    s_mup,
    r_mup,
    s_mdn,
    r_mdn,
    s_rup,
    r_rup,
    s_rdn,
    r_rdn,
    s_gt,
    r_gt,
    s_ge,
    r_ge,
):
    n_edge, n_tile, edges, frames, rows, width, slots = dims
    band = rows * width
    halo = RADIUS * width
    me = lax.axis_index("edge")
    tile = lax.axis_index("tile")
    up, down = tile - 1, tile + 1
    has_up, has_down = tile > 0, tile < n_tile - 1

    barrier = pltpu.get_barrier_semaphore()
    for rel in range(1, n_edge):
        pl.semaphore_signal(
            barrier, inc=1, device_id=((me + rel) % n_edge, tile), device_id_type=MESH
        )
    for rel in range(1, n_tile):
        pl.semaphore_signal(
            barrier, inc=1, device_id=(me, (tile + rel) % n_tile), device_id_type=MESH
        )
    pl.semaphore_wait(barrier, n_edge + n_tile - 2)

    def remote(src, dst, send_sem, recv_sem, edge_id, tile_id):
        return pltpu.make_async_remote_copy(
            src_ref=src,
            dst_ref=dst,
            send_sem=send_sem,
            recv_sem=recv_sem,
            device_id=(edge_id, tile_id),
            device_id_type=MESH,
        )

    def meta_copy(rel):
        return remote(
            meta_in, meta_all.at[me], s_meta.at[rel], r_meta.at[rel], (me + rel) % n_edge, tile
        )

    for rel in range(1, n_edge):
        meta_copy(rel).start()

    def hid_up(e):
        return remote(
            hidden.at[e, pl.ds(0, width)], hext.at[e, pl.ds(width + band, width)],
            s_hup.at[e], r_hup.at[e], me, up,
        )

    def hid_dn(e):
        return remote(
            hidden.at[e, pl.ds(band - width, width)], hext.at[e, pl.ds(0, width)],
            s_hdn.at[e], r_hdn.at[e], me, down,
        )

    def row_up(buf, s, r, e):
        return remote(
            buf.at[e, pl.ds(width, width)], buf.at[e, pl.ds(width + band, width)],
            s.at[e], r.at[e], me, up,
        )

    def row_dn(buf, s, r, e):
        return remote(
            buf.at[e, pl.ds(band, width)], buf.at[e, pl.ds(0, width)],
            s.at[e], r.at[e], me, down,
        )

    def txt_up(k):
        return remote(
            text.at[k, pl.ds(halo, halo)], text.at[k, pl.ds(halo + band, halo)],
            s_tup.at[k], r_tup.at[k], me, up,
        )

    def txt_dn(k):
        return remote(
            text.at[k, pl.ds(band, halo)], text.at[k, pl.ds(0, halo)],
            s_tdn.at[k], r_tdn.at[k], me, down,
        )

    def start_pair(make_up, make_dn):
        @pl.when(has_up)
        def _():
            make_up.start()

        @pl.when(has_down)
        def _():
            make_dn.start()

    def recv_pair(make_up, make_dn):
        @pl.when(has_down)
        def _():
            make_up.wait_recv()

        @pl.when(has_up)
        def _():
            make_dn.wait_recv()

    def sent_pair(make_up, make_dn):
        @pl.when(has_up)
        def _():
            make_up.wait_send()

        @pl.when(has_down)
        def _():
            make_dn.wait_send()

    def each(count, body):
        def step(i, carry):
            body(i)
            return carry

        lax.fori_loop(0, count, step, 0)

    each(edges, lambda e: start_pair(hid_up(e), hid_dn(e)))

    zero_row = jnp.zeros((width, 128), BF)
    zero_halo = jnp.zeros((halo, 128), BF)

    @pl.when(tile == 0)
    def _():
        def clear(e):
            for buf in (hext, mext, rext):
                buf[e, pl.ds(0, width)] = zero_row

        each(edges, clear)

        def clear_text(k):
            text[k, pl.ds(0, halo)] = zero_halo

        each(n_edge * slots, clear_text)

    @pl.when(tile == n_tile - 1)
    def _():
        def clear(e):
            for buf in (hext, mext, rext):
                buf[e, pl.ds(width + band, width)] = zero_row

        each(edges, clear)

        def clear_text(k):
            text[k, pl.ds(halo + band, halo)] = zero_halo

        each(n_edge * slots, clear_text)

    if (rows + 2 * RADIUS) % 2:

        def clear_pad(k):
            text[k, pl.ds(band + 2 * halo, width)] = zero_row

        each(n_edge * slots, clear_pad)

    meta_all[me] = meta_in[...]
    for rel in range(1, n_edge):
        remote(
            meta_in, meta_all.at[(me - rel + n_edge) % n_edge], s_meta.at[rel], r_meta.at[rel],
            (me + rel) % n_edge, tile,
        ).wait_recv()
    local = pltpu.make_async_copy(meta_all, meta_s, l_meta)
    local.start()
    local.wait()

    def asked(peer):
        picks = [jnp.int32(0)] * slots
        rank = jnp.int32(0)
        for k in range(edges):
            hit = (meta_s[peer, 0, k] == me).astype(jnp.int32)
            goal = meta_s[peer, 0, 8 + k]
            for s in range(slots):
                picks[s] = jnp.where((hit == 1) & (rank == s), goal, picks[s])
            rank = rank + hit
        return picks

    def feat_copy(rel, s):
        return remote(
            send.at[(rel - 1) * slots + s],
            text.at[rel * slots + s, pl.ds(halo, band)],
            s_feat.at[rel * slots + s],
            r_feat.at[rel * slots + s],
            (me - rel + n_edge) % n_edge,
            tile,
        )

    asks = [asked((me - rel + n_edge) % n_edge) for rel in range(n_edge)]
    for s in range(slots):
        for rel in range(1, n_edge):
            send[(rel - 1) * slots + s] = feat[asks[rel][s]]
        for rel in range(1, n_edge):
            feat_copy(rel, s).start()
    for s in range(slots):
        text[s, pl.ds(halo, band)] = feat[asks[0][s]]
    for s in range(slots):
        start_pair(txt_up(s), txt_dn(s))

    for a in range(3):
        for b in range(3):
            at = pl.ds((a * 3 + b) * 128, 128)
            wh[at, :] = gate_w[a, b, 0:128, :]
            wm[at, 0:256] = gate_w[a, b, 128:256, :]
            wm[at, 256:384] = cand_w[a, b, 128:256, :]
            wr[at, :] = cand_w[a, b, 0:128, :]

    col = iota((band + 2 * width, 128), 0) & (width - 1)

    def shifted(buf, e):
        value = buf[e]
        wide = value.astype(F32)
        left = jnp.where(col == 0, 0.0, pltpu.roll(wide, 1, 0)).astype(BF)
        right = jnp.where(
            col == width - 1, 0.0, pltpu.roll(wide, band + 2 * width - 1, 0)
        ).astype(BF)
        x3[:, 0:128] = left
        x3[:, 128:256] = value
        x3[:, 256:384] = right
        return jnp.concatenate(
            [x3[0:band], x3[width : width + band], x3[2 * width : 2 * width + band]], axis=1
        )

    flip_row, flip_col = iota((2 * width, 2 * width), 0), iota((2 * width, 2 * width), 1)
    flip = (
        ((flip_row >= width) == (flip_col >= width))
        & ((flip_row & (width - 1)) + (flip_col & (width - 1)) == width - 1)
    ).astype(F32).astype(BF)

    def flipped(value):
        count = value.shape[0]
        return nn(flip[0:count, 0:count], value).astype(BF)

    def state_part(e):
        source = feat[meta_s[me, 0, 16 + e]]
        for first in range(0, rows, 2):
            last = min(rows, first + 2) * width
            sref[e, pl.ds(first * width, last - first * width)] = flipped(
                source[first * width : last]
            )
        hext[e, pl.ds(width, band)] = hidden[e]
        recv_pair(hid_up(e), hid_dn(e))
        gpre[e] = nn(shifted(hext, e), wh[...])

    each(edges, state_part)

    for s in range(slots):
        for rel in range(1, n_edge):
            feat_copy(rel, s).wait_recv()
            start_pair(txt_up(rel * slots + s), txt_dn(rel * slots + s))
    each(n_edge * slots, lambda k: recv_pair(txt_up(k), txt_dn(k)))

    lane = iota((width, 128), 1)
    place = (width - 1 - iota((width, 128), 0)) + ((lane + 97) & 63) - 32
    inside = (place >= 0) & (place < width)
    scale = 128.0 ** (-0.5)

    def slot_of(e):
        mine = meta_s[me, 0, e]
        rank = jnp.int32(0)
        for k in range(edges):
            rank = rank + jnp.where((meta_s[me, 0, k] == mine) & (k < e), 1, 0)
        return ((mine - me + n_edge) % n_edge) * slots + jnp.minimum(rank, slots - 1)

    def motion(e):
        k = slot_of(e)
        source = sref[e]
        target = text[k]
        for first in range(0, rows, 2):
            count = min(2, rows - first)
            table = nt(
                source[first * width : (first + count) * width],
                target[first * width : (first + 8) * width],
            )
            values = []
            for par in range(count):
                parts = []
                for g in range(4):
                    piece = table[par * width : (par + 1) * width, g * 128 : (g + 1) * 128]
                    moved = pltpu.roll(piece, 0, 1, stride=1, stride_axis=0)
                    parts.append(jnp.where(inside, moved * scale, 0.0).astype(BF))
                value = nn(jnp.concatenate(parts, axis=1), corr_w[par])
                values.append(jnp.maximum(value, 0.0).astype(BF))
            mext[e, pl.ds((first + 1) * width, count * width)] = flipped(
                jnp.concatenate(values, axis=0)
            )
        start_pair(row_up(mext, s_mup, r_mup, e), row_dn(mext, s_mdn, r_mdn, e))

    each(edges, motion)

    def gates(e):
        recv_pair(row_up(mext, s_mup, r_mup, e), row_dn(mext, s_mdn, r_mdn, e))
        both = nn(shifted(mext, e), wm[...])
        cpre[e] = both[:, 256:384]
        gate = jax.nn.sigmoid(gpre[e] + both[:, 0:256])
        upd[e] = gate[:, 0:128]
        rext[e, pl.ds(width, band)] = (gate[:, 128:256] * hidden[e].astype(F32)).astype(BF)
        start_pair(row_up(rext, s_rup, r_rup, e), row_dn(rext, s_rdn, r_rdn, e))

    each(edges, gates)

    gpart[...] = jnp.zeros_like(gpart)
    lane16 = iota((16, 128), 1)
    row16 = iota((16, 128), 0)

    def finish(e):
        recv_pair(row_up(rext, s_rup, r_rup, e), row_dn(rext, s_rdn, r_rdn, e))
        candidate = jnp.tanh(cpre[e] + nn(shifted(rext, e), wr[...]))
        update = upd[e]
        state = hidden[e]
        fresh = ((1.0 - update) * state.astype(F32) + update * candidate).astype(BF)
        used = (e < meta_s[me, 0, 24]).astype(F32)
        live = jnp.full((band, 128), used) > 0.5
        out_hidden[e] = jnp.where(live, fresh, state)
        heads = nn(fresh, head_w[...])
        jac = heads[:, 0:128]
        weighted = jac * jax.nn.softplus(heads[:, 128:256])
        square = lax.dot_general(
            weighted, jac, (((0,), (0,)), ((), ())), preferred_element_type=F32, precision=HIGH
        )
        other = pltpu.roll(pltpu.roll(square, 116, 0), 116, 1)
        block = (square + other)[0:16] * (used / (MAPH * width))
        block = jnp.where((lane16 < 12) & (row16 < 12), block, 0.0)
        gpart[...] += pltpu.roll(block, e * 16, 1)

    each(edges, finish)

    def tile_copy(rel):
        return remote(
            gpart, gtile.at[tile], s_gt.at[rel], r_gt.at[rel], me, (tile + rel) % n_tile
        )

    for rel in range(1, n_tile):
        tile_copy(rel).start()
    gtile[tile] = gpart[...]
    for rel in range(1, n_tile):
        remote(
            gpart, gtile.at[(tile - rel + n_tile) % n_tile], s_gt.at[rel], r_gt.at[rel],
            me, (tile + rel) % n_tile,
        ).wait_recv()
    total = gtile[0]
    for k in range(1, n_tile):
        total = total + gtile[k]
    gsum[...] = total

    def edge_copy(rel):
        return remote(gsum, gall.at[me], s_ge.at[rel], r_ge.at[rel], (me + rel) % n_edge, tile)

    for rel in range(1, n_edge):
        edge_copy(rel).start()
    gall[me] = total
    for rel in range(1, n_edge):
        remote(
            gsum, gall.at[(me - rel + n_edge) % n_edge], s_ge.at[rel], r_ge.at[rel],
            (me + rel) % n_edge, tile,
        ).wait_recv()

    cam_rows, cam_cols = out_cam.shape
    row_id = iota((cam_rows, 128), 0) + tile * cam_rows
    col_id = iota((cam_cols, 128), 0) + me * cam_cols
    same = (iota((128, 128), 0) >> 4) == (iota((128, 128), 1) >> 4)
    lefts, rights = [], []
    for j in range(n_edge):
        spots = meta_all[j, 1:2, :]
        mine = (col_id == spots).astype(F32)
        left = jnp.concatenate([(row_id == spots).astype(F32), mine], axis=0)
        stack = jnp.concatenate([gall[j]] * 8, axis=0)
        lefts.append(nn(left, jnp.where(same, stack, 0.0), HIGH))
        rights.append(mine)
    placed = nt(jnp.concatenate(lefts, axis=1), jnp.concatenate(rights, axis=1), HIGH)
    cam = placed[0:cam_rows]
    row_frame = sixth(iota((cam_rows, cam_cols), 0) + tile * cam_rows)
    col_frame = sixth(iota((cam_rows, cam_cols), 1) + me * cam_cols)
    out_cam[...] = jnp.where(row_frame == col_frame, 0.0, cam)
    own = placed[cam_rows:]
    own_row = sixth(iota((cam_cols, cam_cols), 0))
    own_col = sixth(iota((cam_cols, cam_cols), 1))
    own = jnp.where(own_row == own_col, own, 0.0)
    wide_row = iota((cam_cols, 128), 0)
    wide_lane = iota((cam_cols, 128), 1)
    row_in = wide_row.astype(F32) - 6.0 * sixth(wide_row)
    lane_of = sixth(wide_lane)
    lane_in = wide_lane.astype(F32) - 6.0 * lane_of
    spread = nn(own, (row_in == lane_in).astype(F32), HIGH)
    spread = jnp.where(row_in == lane_of, spread, 0.0)
    fold = (
        sixth(iota((frames, cam_cols), 1)) == iota((frames, cam_cols), 0).astype(F32)
    ).astype(F32)
    out_diag[...] = nn(fold, spread, HIGH)[:, 0:36]

    for rel in range(1, n_edge):
        meta_copy(rel).wait_send()
        edge_copy(rel).wait_send()
        for s in range(slots):
            feat_copy(rel, s).wait_send()
    for rel in range(1, n_tile):
        tile_copy(rel).wait_send()
    each(n_edge * slots, lambda k: sent_pair(txt_up(k), txt_dn(k)))

    def sent(e):
        sent_pair(hid_up(e), hid_dn(e))
        sent_pair(row_up(mext, s_mup, r_mup, e), row_dn(mext, s_mdn, r_mdn, e))
        sent_pair(row_up(rext, s_rup, r_rup, e), row_dn(rext, s_rdn, r_rdn, e))

    each(edges, sent)


def per_device(
    features,
    hidden_state,
    edge_source,
    edge_owner,
    edge_target,
    edge_counts,
    corr_weight,
    gate_weight,
    candidate_weight,
    jacobian_weight,
    confidence_weight,
):
    n_edge, n_tile = lax.axis_size("edge"), lax.axis_size("tile")
    edges = hidden_state.shape[0]
    frames, rows, width, chan = features.shape
    slots = max(2, (2 * edges + n_edge - 1) // n_edge)
    band = rows * width
    me = lax.axis_index("edge")
    owners = edge_owner[:, 0]

    numbers = jnp.concatenate([owners, edge_target, edge_source, edge_counts])
    numbers = jnp.pad(numbers, (0, 128 - numbers.shape[0]))
    inner = jnp.arange(16)[None, :]
    frame = jnp.where(
        inner < 6, (me * frames + edge_source)[:, None], (owners * frames + edge_target)[:, None]
    )
    spots = jnp.where(inner < 12, frame * 6 + inner % 6, -1).reshape(-1)
    spots = jnp.pad(spots, (0, 128 - spots.shape[0]), constant_values=-1)
    meta = jnp.stack([numbers, spots]).astype(jnp.int32)

    grid = corr_weight.reshape(WINDOW, WINDOW, chan)
    side = 32 - RADIUS
    rest = width - side - WINDOW
    corr_w = jnp.stack(
        [
            jnp.pad(grid, ((0, 1), (side, rest), (0, 0))).reshape(8 * width, chan),
            jnp.pad(grid, ((1, 0), (side, rest), (0, 0))).reshape(8 * width, chan),
        ]
    )
    corr_w = jnp.roll(corr_w.reshape(2, 4, 2 * width, chan), width // 2 - 1, axis=2)
    corr_w = corr_w.reshape(2, 8 * width, chan)
    gap = jnp.zeros((chan, 104), BF)
    head_w = jnp.concatenate(
        [
            jacobian_weight,
            gap,
            jnp.broadcast_to(confidence_weight[:, 0:1], (chan, 12)),
            jnp.broadcast_to(confidence_weight[:, 1:2], (chan, 12)),
            gap,
        ],
        axis=1,
    )
    dims = (n_edge, n_tile, edges, frames, rows, width, slots)
    total_slots = n_edge * slots
    text_rows = rows + 2 * RADIUS
    text_rows = text_rows + text_rows % 2
    ext = band + 2 * width
    dma = pltpu.SemaphoreType.DMA
    vmem = pl.BlockSpec(memory_space=pltpu.VMEM)
    hidden_next, cam, diag = pl.pallas_call(
        functools.partial(kernel, dims),
        out_shape=(
            jax.ShapeDtypeStruct((edges, band, chan), BF),
            jax.ShapeDtypeStruct((frames * n_edge * 6 // n_tile, frames * 6), F32),
            jax.ShapeDtypeStruct((frames, 36), F32),
        ),
        in_specs=[vmem] * 7,
        out_specs=(vmem, vmem, vmem),
        scratch_shapes=[
            pltpu.VMEM((n_edge, 2, 128), jnp.int32),
            pltpu.SMEM((n_edge, 2, 128), jnp.int32),
            pltpu.VMEM(((n_edge - 1) * slots, band, chan), BF),
            pltpu.VMEM((total_slots, text_rows * width, chan), BF),
            pltpu.VMEM((edges, band, chan), BF),
            pltpu.VMEM((edges, ext, chan), BF),
            pltpu.VMEM((edges, ext, chan), BF),
            pltpu.VMEM((edges, ext, chan), BF),
            pltpu.VMEM((ext, 3 * chan), BF),
            pltpu.VMEM((9 * chan, 2 * chan), BF),
            pltpu.VMEM((9 * chan, 3 * chan), BF),
            pltpu.VMEM((9 * chan, chan), BF),
            pltpu.VMEM((edges, band, 2 * chan), F32),
            pltpu.VMEM((edges, band, chan), F32),
            pltpu.VMEM((edges, band, chan), F32),
            pltpu.VMEM((16, 128), F32),
            pltpu.VMEM((n_tile, 16, 128), F32),
            pltpu.VMEM((16, 128), F32),
            pltpu.VMEM((n_edge, 16, 128), F32),
            dma((n_edge,)),
            dma((n_edge,)),
            dma,
            dma((total_slots,)),
            dma((total_slots,)),
        ]
        + [dma((total_slots,))] * 4
        + [dma((edges,))] * 12
        + [dma((n_tile,)), dma((n_tile,)), dma((n_edge,)), dma((n_edge,))],
        compiler_params=pltpu.CompilerParams(
            collective_id=0, has_side_effects=True, vmem_limit_bytes=56 * 1024 * 1024
        ),
    )(
        meta,
        features.reshape(frames, band, chan),
        hidden_state.reshape(edges, band, chan),
        corr_w,
        gate_weight,
        candidate_weight,
        head_w,
    )
    return hidden_next.reshape(hidden_state.shape), cam, diag


def solution(mesh):
    placed = (
        P("edge", "tile", None, None),
        P("edge", "tile", None, None),
        P("edge"),
        P("edge", None),
        P("edge"),
        P("edge"),
        P(),
        P(),
        P(),
        P(),
        P(),
    )
    return jax.shard_map(
        per_device,
        mesh=mesh,
        in_specs=placed,
        out_specs=(P("edge", "tile", None, None), P("tile", "edge"), P("edge", None)),
        check_vma=False,
    )
```

```python
import functools

import jax
import jax.numpy as jnp
from jax import lax
from jax.experimental import pallas as pl
from jax.experimental.pallas import tpu as pltpu
from jax.sharding import PartitionSpec as P

MAPH = 48
WINDOW = 7
RADIUS = WINDOW // 2
MESH = pl.DeviceIdType.MESH
HIGH = lax.Precision.HIGHEST
BF = jnp.bfloat16
F32 = jnp.float32


def nt(a, b, precision=None):
    return lax.dot_general(
        a, b, (((1,), (1,)), ((), ())), preferred_element_type=F32, precision=precision
    )


def nn(a, b, precision=None):
    return lax.dot_general(
        a, b, (((1,), (0,)), ((), ())), preferred_element_type=F32, precision=precision
    )


def iota(shape, dim):
    return lax.broadcasted_iota(jnp.int32, shape, dim)


def sixth(index):
    return jnp.floor((index.astype(F32) + 0.5) * (1.0 / 6.0))


def kernel(
    dims,
    meta_in,
    feat_h,
    hidden_h,
    corr_in,
    gate_w,
    cand_w,
    jac_in,
    conf_in,
    out_hidden,
    gall,
    meta_all,
    feat,
    corr_w,
    jall,
    wall,
    meta_s,
    send,
    text,
    sref,
    hext,
    mext,
    rext,
    x3,
    wh,
    wm,
    wr,
    gpre,
    cpre,
    upd,
    gpart,
    gtile,
    gsum,
    l_in,
    l_w,
    s_meta,
    r_meta,
    l_meta,
    s_feat,
    r_feat,
    s_tup,
    r_tup,
    s_tdn,
    r_tdn,
    s_hup,
    r_hup,
    s_hdn,
    r_hdn,
    s_mup,
    r_mup,
    s_mdn,
    r_mdn,
    s_rup,
    r_rup,
    s_rdn,
    r_rdn,
    s_gt,
    r_gt,
    s_ge,
    r_ge,
):
    n_edge, n_tile, edges, frames, rows, width, slots = dims
    band = rows * width
    halo = RADIUS * width
    me = lax.axis_index("edge")
    tile = lax.axis_index("tile")
    up, down = tile - 1, tile + 1
    has_up, has_down = tile > 0, tile < n_tile - 1

    loads = [
        pltpu.make_async_copy(feat_h, feat, l_in.at[0]),
        pltpu.make_async_copy(hidden_h, hext.at[:, pl.ds(width, band)], l_in.at[1]),
    ]
    fills = []
    for a in range(3):
        for b in range(3):
            at = pl.ds((a * 3 + b) * 128, 128)
            first, second = pl.ds(0, 128), pl.ds(128, 128)
            pairs = (
                (gate_w.at[a, b, first], wh.at[at]),
                (gate_w.at[a, b, second], wm.at[at, pl.ds(0, 256)]),
                (cand_w.at[a, b, second], wm.at[at, pl.ds(256, 128)]),
                (cand_w.at[a, b, first], wr.at[at]),
            )
            for source, target in pairs:
                fills.append(pltpu.make_async_copy(source, target, l_w.at[len(fills)]))
    for load in loads + fills:
        load.start()

    barrier = pltpu.get_barrier_semaphore()
    for rel in range(1, n_edge):
        pl.semaphore_signal(
            barrier, inc=1, device_id=((me + rel) % n_edge, tile), device_id_type=MESH
        )
    for rel in range(1, n_tile):
        pl.semaphore_signal(
            barrier, inc=1, device_id=(me, (tile + rel) % n_tile), device_id_type=MESH
        )
    pl.semaphore_wait(barrier, n_edge + n_tile - 2)

    def remote(src, dst, send_sem, recv_sem, edge_id, tile_id):
        return pltpu.make_async_remote_copy(
            src_ref=src,
            dst_ref=dst,
            send_sem=send_sem,
            recv_sem=recv_sem,
            device_id=(edge_id, tile_id),
            device_id_type=MESH,
        )

    def meta_copy(rel):
        return remote(
            meta_in, meta_all.at[me], s_meta.at[rel], r_meta.at[rel], (me + rel) % n_edge, tile
        )

    for rel in range(1, n_edge):
        meta_copy(rel).start()

    def hid_up(e):
        return remote(
            hidden_h.at[e, pl.ds(0, width)], hext.at[e, pl.ds(width + band, width)],
            s_hup.at[e], r_hup.at[e], me, up,
        )

    def hid_dn(e):
        return remote(
            hidden_h.at[e, pl.ds(band - width, width)], hext.at[e, pl.ds(0, width)],
            s_hdn.at[e], r_hdn.at[e], me, down,
        )

    def row_up(buf, s, r, e):
        return remote(
            buf.at[e, pl.ds(width, width)], buf.at[e, pl.ds(width + band, width)],
            s.at[e], r.at[e], me, up,
        )

    def row_dn(buf, s, r, e):
        return remote(
            buf.at[e, pl.ds(band, width)], buf.at[e, pl.ds(0, width)],
            s.at[e], r.at[e], me, down,
        )

    def txt_up(k):
        return remote(
            text.at[k, pl.ds(halo, halo)], text.at[k, pl.ds(halo + band, halo)],
            s_tup.at[k], r_tup.at[k], me, up,
        )

    def txt_dn(k):
        return remote(
            text.at[k, pl.ds(band, halo)], text.at[k, pl.ds(0, halo)],
            s_tdn.at[k], r_tdn.at[k], me, down,
        )

    def start_pair(make_up, make_dn):
        @pl.when(has_up)
        def _():
            make_up.start()

        @pl.when(has_down)
        def _():
            make_dn.start()

    def recv_pair(make_up, make_dn):
        @pl.when(has_down)
        def _():
            make_up.wait_recv()

        @pl.when(has_up)
        def _():
            make_dn.wait_recv()

    def sent_pair(make_up, make_dn):
        @pl.when(has_up)
        def _():
            make_up.wait_send()

        @pl.when(has_down)
        def _():
            make_dn.wait_send()

    def each(count, body):
        def step(i, carry):
            body(i)
            return carry

        lax.fori_loop(0, count, step, 0)

    each(edges, lambda e: start_pair(hid_up(e), hid_dn(e)))

    zero_row = jnp.zeros((width, 128), BF)
    zero_halo = jnp.zeros((halo, 128), BF)

    @pl.when(tile == 0)
    def _():
        def clear(e):
            for buf in (hext, mext, rext):
                buf[e, pl.ds(0, width)] = zero_row

        each(edges, clear)

        def clear_text(k):
            text[k, pl.ds(0, halo)] = zero_halo

        each(n_edge * slots, clear_text)

    @pl.when(tile == n_tile - 1)
    def _():
        def clear(e):
            for buf in (hext, mext, rext):
                buf[e, pl.ds(width + band, width)] = zero_row

        each(edges, clear)

        def clear_text(k):
            text[k, pl.ds(halo + band, halo)] = zero_halo

        each(n_edge * slots, clear_text)

    if (rows + 2 * RADIUS) % 2:

        def clear_pad(k):
            text[k, pl.ds(band + 2 * halo, width)] = zero_row

        each(n_edge * slots, clear_pad)

    spot = iota((2 * width, 64), 0)
    rank = ((spot + 97) & 63) - 32
    second = ((spot + 97) & 127) >> 6
    names = iota((2 * width, 64), 1)
    lookup = jnp.concatenate(
        [corr_in[...].astype(F32), jnp.zeros((64 - WINDOW * WINDOW, 128), F32)], axis=0
    ).astype(BF)
    for par in range(2):
        for g in range(4):
            down_by = 2 * g - par + second
            fits = (rank >= -RADIUS) & (rank <= RADIUS) & (down_by >= 0) & (down_by < WINDOW)
            pick = (names == down_by * WINDOW + rank + RADIUS) & fits
            corr_w[par, pl.ds(g * 2 * width, 2 * width)] = nn(
                pick.astype(F32).astype(BF), lookup
            ).astype(BF)

    place12 = iota((32, 64), 0)
    which = place12 >> 4
    within = place12 & 15
    name12 = iota((32, 64), 1)
    pick_j = (within < 12) & (name12 == which * 12 + within)
    pick_c = (within < 12) & (name12 == 24 + which)
    both_heads = jnp.concatenate(
        [jac_in[...].astype(F32), conf_in[...].astype(F32), jnp.zeros((32, 128), F32)], axis=0
    ).astype(BF)
    picks_all = jnp.concatenate([pick_j.astype(F32), pick_c.astype(F32)], axis=0).astype(BF)
    head_w = nn(picks_all, both_heads).astype(BF)

    meta_all[me] = meta_in[...]
    for rel in range(1, n_edge):
        remote(
            meta_in, meta_all.at[(me - rel + n_edge) % n_edge], s_meta.at[rel], r_meta.at[rel],
            (me + rel) % n_edge, tile,
        ).wait_recv()
    loads[0].wait()
    local = pltpu.make_async_copy(meta_all, meta_s, l_meta)
    local.start()
    local.wait()

    def asked(peer):
        picks = [jnp.int32(0)] * slots
        rank = jnp.int32(0)
        for k in range(edges):
            hit = (meta_s[peer, 0, k] == me).astype(jnp.int32)
            goal = meta_s[peer, 0, 8 + k]
            for s in range(slots):
                picks[s] = jnp.where((hit == 1) & (rank == s), goal, picks[s])
            rank = rank + hit
        return picks

    def feat_copy(rel, s):
        return remote(
            send.at[(rel - 1) * slots + s],
            text.at[rel * slots + s, pl.ds(halo, band)],
            s_feat.at[rel * slots + s],
            r_feat.at[rel * slots + s],
            (me - rel + n_edge) % n_edge,
            tile,
        )

    asks = [asked((me - rel + n_edge) % n_edge) for rel in range(n_edge)]
    for s in range(slots):
        for rel in range(1, n_edge):
            send[(rel - 1) * slots + s] = feat[asks[rel][s]]
        for rel in range(1, n_edge):
            feat_copy(rel, s).start()
    for s in range(slots):
        text[s, pl.ds(halo, band)] = feat[asks[0][s]]
    for s in range(slots):
        start_pair(txt_up(s), txt_dn(s))

    col = iota((band + 2 * width, 128), 0) & (width - 1)

    def shifted(buf, e):
        value = buf[e]
        wide = value.astype(F32)
        left = jnp.where(col == 0, 0.0, pltpu.roll(wide, 1, 0)).astype(BF)
        right = jnp.where(
            col == width - 1, 0.0, pltpu.roll(wide, band + 2 * width - 1, 0)
        ).astype(BF)
        x3[:, 0:128] = left
        x3[:, 128:256] = value
        x3[:, 256:384] = right
        return jnp.concatenate(
            [x3[0:band], x3[width : width + band], x3[2 * width : 2 * width + band]], axis=1
        )

    flip_row, flip_col = iota((2 * width, 2 * width), 0), iota((2 * width, 2 * width), 1)
    flip = (
        ((flip_row >= width) == (flip_col >= width))
        & ((flip_row & (width - 1)) + (flip_col & (width - 1)) == width - 1)
    ).astype(F32).astype(BF)

    def flipped(value):
        count = value.shape[0]
        return nn(flip[0:count, 0:count], value).astype(BF)

    def state_part(e):
        source = feat[meta_s[me, 0, 16 + e]]
        for first in range(0, rows, 2):
            last = min(rows, first + 2) * width
            sref[e, pl.ds(first * width, last - first * width)] = flipped(
                source[first * width : last]
            )
        recv_pair(hid_up(e), hid_dn(e))
        gpre[e] = nn(shifted(hext, e), wh[...])

    loads[1].wait()
    for fill in fills:
        fill.wait()
    each(edges, state_part)

    for s in range(slots):
        for rel in range(1, n_edge):
            feat_copy(rel, s).wait_recv()
            start_pair(txt_up(rel * slots + s), txt_dn(rel * slots + s))
    each(n_edge * slots, lambda k: recv_pair(txt_up(k), txt_dn(k)))

    lane = iota((width, 128), 1)
    place = (width - 1 - iota((width, 128), 0)) + ((lane + 97) & 63) - 32
    inside = (place >= 0) & (place < width)
    scale = 128.0 ** (-0.5)

    def slot_of(e):
        mine = meta_s[me, 0, e]
        rank = jnp.int32(0)
        for k in range(edges):
            rank = rank + jnp.where((meta_s[me, 0, k] == mine) & (k < e), 1, 0)
        return ((mine - me + n_edge) % n_edge) * slots + jnp.minimum(rank, slots - 1)

    def motion(e):
        k = slot_of(e)
        source = sref[e]
        target = text[k]
        for first in range(0, rows, 2):
            count = min(2, rows - first)
            table = nt(
                source[first * width : (first + count) * width],
                target[first * width : (first + 8) * width],
            )
            values = []
            for par in range(count):
                parts = []
                for g in range(4):
                    piece = table[par * width : (par + 1) * width, g * 128 : (g + 1) * 128]
                    moved = pltpu.roll(piece, 0, 1, stride=1, stride_axis=0)
                    parts.append(jnp.where(inside, moved * scale, 0.0).astype(BF))
                value = nn(jnp.concatenate(parts, axis=1), corr_w[par])
                values.append(jnp.maximum(value, 0.0).astype(BF))
            mext[e, pl.ds((first + 1) * width, count * width)] = flipped(
                jnp.concatenate(values, axis=0)
            )
        start_pair(row_up(mext, s_mup, r_mup, e), row_dn(mext, s_mdn, r_mdn, e))

    each(edges, motion)

    def gates(e):
        recv_pair(row_up(mext, s_mup, r_mup, e), row_dn(mext, s_mdn, r_mdn, e))
        both = nn(shifted(mext, e), wm[...])
        cpre[e] = both[:, 256:384]
        gate = jax.nn.sigmoid(gpre[e] + both[:, 0:256])
        upd[e] = gate[:, 0:128]
        rext[e, pl.ds(width, band)] = (gate[:, 128:256] * hext[e, pl.ds(width, band)].astype(F32)).astype(BF)
        start_pair(row_up(rext, s_rup, r_rup, e), row_dn(rext, s_rdn, r_rdn, e))

    each(edges, gates)

    def finish(e):
        recv_pair(row_up(rext, s_rup, r_rup, e), row_dn(rext, s_rdn, r_rdn, e))
        candidate = jnp.tanh(cpre[e] + nn(shifted(rext, e), wr[...]))
        update = upd[e]
        state = hext[e, pl.ds(width, band)]
        fresh = ((1.0 - update) * state.astype(F32) + update * candidate).astype(BF)
        used = (e < meta_s[me, 0, 24]).astype(F32)
        live = jnp.full((band, 128), used) > 0.5
        out_hidden[e] = jnp.where(live, fresh, state)
        heads = nt(head_w, fresh)
        jac = heads[0:32]
        weighted = jac * jax.nn.softplus(heads[32:64])
        at16 = pl.ds(pl.multiple_of(e * 16, 16), 16)
        jall[at16] = jnp.concatenate([jac[0:16], jac[16:32]], axis=1).astype(BF)
        wall[at16] = jnp.concatenate([weighted[0:16], weighted[16:32]], axis=1).astype(BF)

    each(edges, finish)

    same = (iota((128, 128), 0) >> 4) == (iota((128, 128), 1) >> 4)
    square = jnp.where(same, nt(wall[...], jall[...]), 0.0)
    blocks = square[0:16]
    for e in range(1, edges):
        blocks = blocks + square[e * 16 : (e + 1) * 16]
    alive = (iota((16, 128), 1) >> 4) < meta_s[me, 0, 24]
    gpart[...] = jnp.where(alive, blocks * (1.0 / (MAPH * width)), 0.0)

    def tile_copy(rel):
        return remote(
            gpart, gtile.at[tile], s_gt.at[rel], r_gt.at[rel], me, (tile + rel) % n_tile
        )

    for rel in range(1, n_tile):
        tile_copy(rel).start()
    gtile[tile] = gpart[...]
    for rel in range(1, n_tile):
        remote(
            gpart, gtile.at[(tile - rel + n_tile) % n_tile], s_gt.at[rel], r_gt.at[rel],
            me, (tile + rel) % n_tile,
        ).wait_recv()
    total = gtile[0]
    for k in range(1, n_tile):
        total = total + gtile[k]
    gsum[...] = total

    def edge_copy(rel):
        return remote(gsum, gall.at[me], s_ge.at[rel], r_ge.at[rel], (me + rel) % n_edge, tile)

    for rel in range(1, n_edge):
        edge_copy(rel).start()
    gall[me] = total
    for rel in range(1, n_edge):
        remote(
            gsum, gall.at[(me - rel + n_edge) % n_edge], s_ge.at[rel], r_ge.at[rel],
            (me + rel) % n_edge, tile,
        ).wait_recv()

    for rel in range(1, n_edge):
        meta_copy(rel).wait_send()
        edge_copy(rel).wait_send()
        for s in range(slots):
            feat_copy(rel, s).wait_send()
    for rel in range(1, n_tile):
        tile_copy(rel).wait_send()
    each(n_edge * slots, lambda k: sent_pair(txt_up(k), txt_dn(k)))

    def sent(e):
        sent_pair(hid_up(e), hid_dn(e))
        sent_pair(row_up(mext, s_mup, r_mup, e), row_dn(mext, s_mdn, r_mdn, e))
        sent_pair(row_up(rext, s_rup, r_rup, e), row_dn(rext, s_rdn, r_rdn, e))

    each(edges, sent)


def halves(value):
    high = value.astype(BF)
    return high, (value - high.astype(F32)).astype(BF)


def assemble(dims, meta_s, gall, hidden_h, out_hidden, out_cam, out_diag, held, sem):
    n_edge, n_tile, edges, frames, rows, width, slots = dims
    fetch = pltpu.make_async_copy(hidden_h, held, sem.at[0])
    fetch.start()
    me = lax.axis_index("edge")
    tile = lax.axis_index("tile")
    cam_rows, cam_cols = out_cam.shape
    row_id = iota((cam_rows, 128), 0) + tile * cam_rows
    col_id = iota((cam_cols, 128), 0) + me * cam_cols
    same = (iota((128, 128), 0) >> 4) == (iota((128, 128), 1) >> 4)
    lane = iota((1, 128), 1)
    inner = lane & 15
    digit = jnp.where(inner < 6, inner, inner - 6)
    lefts, lows, rights = [], [], []
    for j in range(n_edge):
        spots = jnp.full((1, 128), -1, jnp.int32)
        for e in range(edges):
            source = (j * frames + meta_s[j, 0, 16 + e]) * 6
            target = (meta_s[j, 0, e] * frames + meta_s[j, 0, 8 + e]) * 6
            here = jnp.where(inner < 6, source, target) + digit
            spots = jnp.where(((lane >> 4) == e) & (inner < 12), here, spots)
        mine = (col_id == spots).astype(F32)
        left = jnp.concatenate([(row_id == spots).astype(F32), mine], axis=0).astype(BF)
        stack = jnp.where(same, jnp.concatenate([gall[j]] * 8, axis=0), 0.0)
        picked = nn(
            jnp.concatenate([left, left], axis=1), jnp.concatenate(halves(stack), axis=0)
        )
        high, low = halves(picked)
        lefts.append(high)
        lows.append(low)
        rights.append(mine.astype(BF))
    placed = nt(jnp.concatenate(lefts + lows, axis=1), jnp.concatenate(rights + rights, axis=1))
    fetch.wait()
    store = pltpu.make_async_copy(held, out_hidden, sem.at[1])
    store.start()
    cam = placed[0:cam_rows]
    row_frame = sixth(iota((cam_rows, cam_cols), 0) + tile * cam_rows)
    col_frame = sixth(iota((cam_rows, cam_cols), 1) + me * cam_cols)
    out_cam[...] = jnp.where(row_frame == col_frame, 0.0, cam)
    own = placed[cam_rows:]
    own_row = sixth(iota((cam_cols, cam_cols), 0))
    own_col = sixth(iota((cam_cols, cam_cols), 1))
    own = jnp.where(own_row == own_col, own, 0.0)
    wide_row = iota((cam_cols, 128), 0)
    wide_lane = iota((cam_cols, 128), 1)
    row_in = wide_row.astype(F32) - 6.0 * sixth(wide_row)
    lane_of = sixth(wide_lane)
    lane_in = wide_lane.astype(F32) - 6.0 * lane_of
    gather = (row_in == lane_in).astype(F32).astype(BF)
    high, low = halves(own)
    spread = jnp.where(row_in == lane_of, nn(high, gather) + nn(low, gather), 0.0)
    fold = (
        sixth(iota((frames, cam_cols), 1)) == iota((frames, cam_cols), 0).astype(F32)
    ).astype(F32).astype(BF)
    high, low = halves(spread)
    out_diag[...] = (nn(fold, high) + nn(fold, low))[:, 0:36]
    store.wait()


def per_device(
    features,
    hidden_state,
    edge_source,
    edge_owner,
    edge_target,
    edge_counts,
    corr_weight,
    gate_weight,
    candidate_weight,
    jacobian_weight,
    confidence_weight,
):
    n_edge, n_tile = lax.axis_size("edge"), lax.axis_size("tile")
    edges = hidden_state.shape[0]
    frames, rows, width, chan = features.shape
    slots = max(2, (2 * edges + n_edge - 1) // n_edge)
    band = rows * width
    owners = edge_owner[:, 0]

    numbers = jnp.concatenate([owners, edge_target, edge_source, edge_counts])
    numbers = jnp.pad(numbers, (0, 128 - numbers.shape[0]))
    meta = numbers[None, :].astype(jnp.int32)
    dims = (n_edge, n_tile, edges, frames, rows, width, slots)
    total_slots = n_edge * slots
    text_rows = rows + 2 * RADIUS
    text_rows = text_rows + text_rows % 2
    ext = band + 2 * width
    dma = pltpu.SemaphoreType.DMA
    vmem = pl.BlockSpec(memory_space=pltpu.VMEM)
    hbm = pl.BlockSpec(memory_space=pl.ANY)
    state, gall, meta_all = pl.pallas_call(
        functools.partial(kernel, dims),
        out_shape=(
            jax.ShapeDtypeStruct((edges, band, chan), BF),
            jax.ShapeDtypeStruct((n_edge, 16, 128), F32),
            jax.ShapeDtypeStruct((n_edge, 1, 128), jnp.int32),
        ),
        in_specs=[vmem, hbm, hbm, vmem, hbm, hbm, vmem, vmem],
        out_specs=(vmem, vmem, vmem),
        scratch_shapes=[
            pltpu.VMEM((frames, band, chan), BF),
            pltpu.VMEM((2, 8 * width, chan), BF),
            pltpu.VMEM((edges * 16, 2 * band), BF),
            pltpu.VMEM((edges * 16, 2 * band), BF),
            pltpu.SMEM((n_edge, 1, 128), jnp.int32),
            pltpu.VMEM(((n_edge - 1) * slots, band, chan), BF),
            pltpu.VMEM((total_slots, text_rows * width, chan), BF),
            pltpu.VMEM((edges, band, chan), BF),
            pltpu.VMEM((edges, ext, chan), BF),
            pltpu.VMEM((edges, ext, chan), BF),
            pltpu.VMEM((edges, ext, chan), BF),
            pltpu.VMEM((ext, 3 * chan), BF),
            pltpu.VMEM((9 * chan, 2 * chan), BF),
            pltpu.VMEM((9 * chan, 3 * chan), BF),
            pltpu.VMEM((9 * chan, chan), BF),
            pltpu.VMEM((edges, band, 2 * chan), F32),
            pltpu.VMEM((edges, band, chan), F32),
            pltpu.VMEM((edges, band, chan), F32),
            pltpu.VMEM((16, 128), F32),
            pltpu.VMEM((n_tile, 16, 128), F32),
            pltpu.VMEM((16, 128), F32),
            dma((2,)),
            dma((36,)),
            dma((n_edge,)),
            dma((n_edge,)),
            dma,
            dma((total_slots,)),
            dma((total_slots,)),
        ]
        + [dma((total_slots,))] * 4
        + [dma((edges,))] * 12
        + [dma((n_tile,)), dma((n_tile,)), dma((n_edge,)), dma((n_edge,))],
        compiler_params=pltpu.CompilerParams(
            collective_id=0, has_side_effects=True, vmem_limit_bytes=56 * 1024 * 1024
        ),
    )(
        meta,
        features.reshape(frames, band, chan),
        hidden_state.reshape(edges, band, chan),
        corr_weight,
        gate_weight,
        candidate_weight,
        jacobian_weight.T,
        jnp.pad(confidence_weight.T, ((0, 6), (0, 0))),
    )
    hidden_next, cam, diag = pl.pallas_call(
        functools.partial(assemble, dims),
        out_shape=(
            jax.ShapeDtypeStruct((edges, band, chan), BF),
            jax.ShapeDtypeStruct((frames * n_edge * 6 // n_tile, frames * 6), F32),
            jax.ShapeDtypeStruct((frames, 36), F32),
        ),
        in_specs=[pl.BlockSpec(memory_space=pltpu.SMEM), vmem, hbm],
        out_specs=(hbm, vmem, vmem),
        scratch_shapes=[pltpu.VMEM((edges, band, chan), BF), dma((2,))],
    )(meta_all, gall, state)
    return hidden_next.reshape(hidden_state.shape), cam, diag


def solution(mesh):
    placed = (
        P("edge", "tile", None, None),
        P("edge", "tile", None, None),
        P("edge"),
        P("edge", None),
        P("edge"),
        P("edge"),
        P(),
        P(),
        P(),
        P(),
        P(),
    )
    return jax.shard_map(
        per_device,
        mesh=mesh,
        in_specs=placed,
        out_specs=(P("edge", "tile", None, None), P("tile", "edge"), P("edge", None)),
        check_vma=False,
    )
```

```python
import functools

import jax
import jax.numpy as jnp
from jax import lax
from jax.experimental import pallas as pl
from jax.experimental.pallas import tpu as pltpu
from jax.sharding import PartitionSpec as P

MAPH = 48
WINDOW = 7
RADIUS = WINDOW // 2
MESH = pl.DeviceIdType.MESH
HIGH = lax.Precision.HIGHEST
BF = jnp.bfloat16
F32 = jnp.float32


def nt(a, b, precision=None):
    return lax.dot_general(
        a, b, (((1,), (1,)), ((), ())), preferred_element_type=F32, precision=precision
    )


def nn(a, b, precision=None):
    return lax.dot_general(
        a, b, (((1,), (0,)), ((), ())), preferred_element_type=F32, precision=precision
    )


def iota(shape, dim):
    return lax.broadcasted_iota(jnp.int32, shape, dim)


def sixth(index):
    return jnp.floor((index.astype(F32) + 0.5) * (1.0 / 6.0))


def kernel(
    dims,
    meta_in,
    feat_h,
    hidden_h,
    corr_in,
    gate_w,
    cand_w,
    jac_in,
    conf_in,
    out_hidden,
    gall,
    meta_all,
    feat,
    corr_w,
    jall,
    wall,
    meta_s,
    send,
    text,
    sref,
    hext,
    mext,
    rext,
    x3,
    wh,
    wm,
    wr,
    gpre,
    cpre,
    upd,
    gpart,
    gtile,
    gsum,
    l_in,
    l_w,
    s_meta,
    r_meta,
    l_meta,
    s_feat,
    r_feat,
    s_tup,
    r_tup,
    s_tdn,
    r_tdn,
    s_hup,
    r_hup,
    s_hdn,
    r_hdn,
    s_mup,
    r_mup,
    s_mdn,
    r_mdn,
    s_rup,
    r_rup,
    s_rdn,
    r_rdn,
    s_gt,
    r_gt,
    s_ge,
    r_ge,
):
    n_edge, n_tile, edges, frames, rows, width, slots = dims
    band = rows * width
    halo = RADIUS * width
    me = lax.axis_index("edge")
    tile = lax.axis_index("tile")
    up, down = tile - 1, tile + 1
    has_up, has_down = tile > 0, tile < n_tile - 1

    loads = [
        pltpu.make_async_copy(feat_h, feat, l_in.at[0]),
        pltpu.make_async_copy(hidden_h, hext.at[:, pl.ds(width, band)], l_in.at[1]),
    ]
    fills = []
    for a in range(3):
        for b in range(3):
            at = pl.ds((a * 3 + b) * 128, 128)
            first, second = pl.ds(0, 128), pl.ds(128, 128)
            pairs = (
                (gate_w.at[a, b, first], wh.at[at]),
                (gate_w.at[a, b, second], wm.at[at, pl.ds(0, 256)]),
                (cand_w.at[a, b, second], wm.at[at, pl.ds(256, 128)]),
                (cand_w.at[a, b, first], wr.at[at]),
            )
            for source, target in pairs:
                fills.append(pltpu.make_async_copy(source, target, l_w.at[len(fills)]))
    for load in loads + fills:
        load.start()

    barrier = pltpu.get_barrier_semaphore()
    for rel in range(1, n_edge):
        pl.semaphore_signal(
            barrier, inc=1, device_id=((me + rel) % n_edge, tile), device_id_type=MESH
        )
    for rel in range(1, n_tile):
        pl.semaphore_signal(
            barrier, inc=1, device_id=(me, (tile + rel) % n_tile), device_id_type=MESH
        )
    pl.semaphore_wait(barrier, n_edge + n_tile - 2)

    def remote(src, dst, send_sem, recv_sem, edge_id, tile_id):
        return pltpu.make_async_remote_copy(
            src_ref=src,
            dst_ref=dst,
            send_sem=send_sem,
            recv_sem=recv_sem,
            device_id=(edge_id, tile_id),
            device_id_type=MESH,
        )

    def meta_copy(rel):
        return remote(
            meta_in, meta_all.at[me], s_meta.at[rel], r_meta.at[rel], (me + rel) % n_edge, tile
        )

    for rel in range(1, n_edge):
        meta_copy(rel).start()

    def hid_up(e):
        return remote(
            hidden_h.at[e, pl.ds(0, width)], hext.at[e, pl.ds(width + band, width)],
            s_hup.at[e], r_hup.at[e], me, up,
        )

    def hid_dn(e):
        return remote(
            hidden_h.at[e, pl.ds(band - width, width)], hext.at[e, pl.ds(0, width)],
            s_hdn.at[e], r_hdn.at[e], me, down,
        )

    def row_up(buf, s, r, e):
        return remote(
            buf.at[e, pl.ds(width, width)], buf.at[e, pl.ds(width + band, width)],
            s.at[e], r.at[e], me, up,
        )

    def row_dn(buf, s, r, e):
        return remote(
            buf.at[e, pl.ds(band, width)], buf.at[e, pl.ds(0, width)],
            s.at[e], r.at[e], me, down,
        )

    def txt_up(k):
        return remote(
            text.at[k, pl.ds(halo, halo)], text.at[k, pl.ds(halo + band, halo)],
            s_tup.at[k], r_tup.at[k], me, up,
        )

    def txt_dn(k):
        return remote(
            text.at[k, pl.ds(band, halo)], text.at[k, pl.ds(0, halo)],
            s_tdn.at[k], r_tdn.at[k], me, down,
        )

    def start_pair(make_up, make_dn):
        @pl.when(has_up)
        def _():
            make_up.start()

        @pl.when(has_down)
        def _():
            make_dn.start()

    def recv_pair(make_up, make_dn):
        @pl.when(has_down)
        def _():
            make_up.wait_recv()

        @pl.when(has_up)
        def _():
            make_dn.wait_recv()

    def sent_pair(make_up, make_dn):
        @pl.when(has_up)
        def _():
            make_up.wait_send()

        @pl.when(has_down)
        def _():
            make_dn.wait_send()

    def each(count, body):
        def step(i, carry):
            body(i)
            return carry

        lax.fori_loop(0, count, step, 0)

    each(edges, lambda e: start_pair(hid_up(e), hid_dn(e)))

    zero_row = jnp.zeros((width, 128), BF)
    zero_halo = jnp.zeros((halo, 128), BF)

    @pl.when(tile == 0)
    def _():
        def clear(e):
            for buf in (hext, mext, rext):
                buf[e, pl.ds(0, width)] = zero_row

        each(edges, clear)

        def clear_text(k):
            text[k, pl.ds(0, halo)] = zero_halo

        each(n_edge * slots, clear_text)

    @pl.when(tile == n_tile - 1)
    def _():
        def clear(e):
            for buf in (hext, mext, rext):
                buf[e, pl.ds(width + band, width)] = zero_row

        each(edges, clear)

        def clear_text(k):
            text[k, pl.ds(halo + band, halo)] = zero_halo

        each(n_edge * slots, clear_text)

    if (rows + 2 * RADIUS) % 2:

        def clear_pad(k):
            text[k, pl.ds(band + 2 * halo, width)] = zero_row

        each(n_edge * slots, clear_pad)

    spot = iota((2 * width, 64), 0)
    rank = ((spot + 97) & 63) - 32
    second = ((spot + 97) & 127) >> 6
    names = iota((2 * width, 64), 1)
    lookup = jnp.concatenate(
        [corr_in[...].astype(F32), jnp.zeros((64 - WINDOW * WINDOW, 128), F32)], axis=0
    ).astype(BF)
    for par in range(2):
        for g in range(4):
            down_by = 2 * g - par + second
            fits = (rank >= -RADIUS) & (rank <= RADIUS) & (down_by >= 0) & (down_by < WINDOW)
            pick = (names == down_by * WINDOW + rank + RADIUS) & fits
            corr_w[par, pl.ds(g * 2 * width, 2 * width)] = nn(
                pick.astype(F32).astype(BF), lookup
            ).astype(BF)

    place12 = iota((32, 64), 0)
    which = place12 >> 4
    within = place12 & 15
    name12 = iota((32, 64), 1)
    pick_j = (within < 12) & (name12 == which * 12 + within)
    padded_jac = jnp.concatenate(
        [jac_in[...].astype(F32), jnp.zeros((40, 128), F32)], axis=0
    ).astype(BF)
    conf_wide = conf_in[...].astype(F32)
    tall = iota((32, 128), 0)
    conf_rows = jnp.where(
        tall < 16,
        jnp.broadcast_to(conf_wide[0:1], (32, 128)),
        jnp.broadcast_to(conf_wide[1:2], (32, 128)),
    )
    head_w = jnp.concatenate(
        [
            nn(pick_j.astype(F32).astype(BF), padded_jac),
            jnp.where((tall & 15) < 12, conf_rows, 0.0),
        ],
        axis=0,
    ).astype(BF)

    meta_all[me] = meta_in[...]
    for rel in range(1, n_edge):
        remote(
            meta_in, meta_all.at[(me - rel + n_edge) % n_edge], s_meta.at[rel], r_meta.at[rel],
            (me + rel) % n_edge, tile,
        ).wait_recv()
    loads[0].wait()
    local = pltpu.make_async_copy(meta_all, meta_s, l_meta)
    local.start()
    local.wait()

    def asked(peer):
        picks = [jnp.int32(0)] * slots
        rank = jnp.int32(0)
        for k in range(edges):
            hit = (meta_s[peer, 0, k] == me).astype(jnp.int32)
            goal = meta_s[peer, 0, 8 + k]
            for s in range(slots):
                picks[s] = jnp.where((hit == 1) & (rank == s), goal, picks[s])
            rank = rank + hit
        return picks

    def feat_copy(rel, s):
        return remote(
            send.at[(rel - 1) * slots + s],
            text.at[rel * slots + s, pl.ds(halo, band)],
            s_feat.at[rel * slots + s],
            r_feat.at[rel * slots + s],
            (me - rel + n_edge) % n_edge,
            tile,
        )

    asks = [asked((me - rel + n_edge) % n_edge) for rel in range(n_edge)]
    for s in range(slots):
        for rel in range(1, n_edge):
            send[(rel - 1) * slots + s] = feat[asks[rel][s]]
        for rel in range(1, n_edge):
            feat_copy(rel, s).start()
    for s in range(slots):
        text[s, pl.ds(halo, band)] = feat[asks[0][s]]
    for s in range(slots):
        start_pair(txt_up(s), txt_dn(s))

    col = iota((band + 2 * width, 128), 0) & (width - 1)

    group = 2 if edges % 2 == 0 else 1

    def shifted(buf, first):
        parts = []
        for q in range(group):
            value = buf[first + q]
            wide = value.astype(F32)
            left = jnp.where(col == 0, 0.0, pltpu.roll(wide, 1, 0)).astype(BF)
            right = jnp.where(
                col == width - 1, 0.0, pltpu.roll(wide, band + 2 * width - 1, 0)
            ).astype(BF)
            x3[q, :, 0:128] = left
            x3[q, :, 128:256] = value
            x3[q, :, 256:384] = right
        for q in range(group):
            parts.append(
                jnp.concatenate(
                    [x3[q, a * width : a * width + band] for a in range(3)], axis=1
                )
            )
        return jnp.concatenate(parts, axis=0)

    def grouped(body):
        each(edges // group, lambda i: body(i * group))

    flip_row, flip_col = iota((2 * width, 2 * width), 0), iota((2 * width, 2 * width), 1)
    flip = (
        ((flip_row >= width) == (flip_col >= width))
        & ((flip_row & (width - 1)) + (flip_col & (width - 1)) == width - 1)
    ).astype(F32).astype(BF)

    def flipped(value):
        count = value.shape[0]
        return nn(flip[0:count, 0:count], value).astype(BF)

    def state_part(e):
        for q in range(group):
            recv_pair(hid_up(e + q), hid_dn(e + q))
        for q in range(group):
            source = feat[meta_s[me, 0, 16 + e + q]]
            for first in range(0, rows, 2):
                last = min(rows, first + 2) * width
                sref[e + q, pl.ds(first * width, last - first * width)] = flipped(
                    source[first * width : last]
                )
        value = nn(shifted(hext, e), wh[...])
        for q in range(group):
            gpre[e + q] = value[q * band : (q + 1) * band]

    loads[1].wait()
    for fill in fills:
        fill.wait()
    grouped(state_part)

    for s in range(slots):
        for rel in range(1, n_edge):
            feat_copy(rel, s).wait_recv()
            start_pair(txt_up(rel * slots + s), txt_dn(rel * slots + s))
    each(n_edge * slots, lambda k: recv_pair(txt_up(k), txt_dn(k)))

    lane = iota((width, 128), 1)
    place = (width - 1 - iota((width, 128), 0)) + ((lane + 97) & 63) - 32
    inside = (place >= 0) & (place < width)
    scale = 128.0 ** (-0.5)

    def slot_of(e):
        mine = meta_s[me, 0, e]
        rank = jnp.int32(0)
        for k in range(edges):
            rank = rank + jnp.where((meta_s[me, 0, k] == mine) & (k < e), 1, 0)
        return ((mine - me + n_edge) % n_edge) * slots + jnp.minimum(rank, slots - 1)

    def motion_of(e):
        k = slot_of(e)
        source = sref[e]
        target = text[k]
        for first in range(0, rows, 2):
            count = min(2, rows - first)
            table = nt(
                source[first * width : (first + count) * width],
                target[first * width : (first + 8) * width],
            )
            values = []
            for par in range(count):
                parts = []
                for g in range(4):
                    piece = table[par * width : (par + 1) * width, g * 128 : (g + 1) * 128]
                    moved = pltpu.roll(piece, 0, 1, stride=1, stride_axis=0)
                    parts.append(jnp.where(inside, moved * scale, 0.0).astype(BF))
                value = nn(jnp.concatenate(parts, axis=1), corr_w[par])
                values.append(jnp.maximum(value, 0.0).astype(BF))
            mext[e, pl.ds((first + 1) * width, count * width)] = flipped(
                jnp.concatenate(values, axis=0)
            )

    def motion(e):
        for q in range(group):
            motion_of(e + q)
        for q in range(group):
            start_pair(
                row_up(mext, s_mup, r_mup, e + q), row_dn(mext, s_mdn, r_mdn, e + q)
            )

    grouped(motion)

    def gates(e):
        for q in range(group):
            recv_pair(
                row_up(mext, s_mup, r_mup, e + q), row_dn(mext, s_mdn, r_mdn, e + q)
            )
        both = nn(shifted(mext, e), wm[...])
        for q in range(group):
            part = both[q * band : (q + 1) * band]
            cpre[e + q] = part[:, 256:384]
            gate = jax.nn.sigmoid(gpre[e + q] + part[:, 0:256])
            upd[e + q] = gate[:, 0:128]
            state = hext[e + q, pl.ds(width, band)].astype(F32)
            rext[e + q, pl.ds(width, band)] = (gate[:, 128:256] * state).astype(BF)
        for q in range(group):
            start_pair(
                row_up(rext, s_rup, r_rup, e + q), row_dn(rext, s_rdn, r_rdn, e + q)
            )

    grouped(gates)

    def finish(e):
        for q in range(group):
            recv_pair(
                row_up(rext, s_rup, r_rup, e + q), row_dn(rext, s_rdn, r_rdn, e + q)
            )
        mixed = nn(shifted(rext, e), wr[...])
        for q in range(group):
            candidate = jnp.tanh(cpre[e + q] + mixed[q * band : (q + 1) * band])
            update = upd[e + q]
            state = hext[e + q, pl.ds(width, band)]
            fresh = ((1.0 - update) * state.astype(F32) + update * candidate).astype(BF)
            used = (e + q < meta_s[me, 0, 24]).astype(F32)
            live = jnp.full((band, 128), used) > 0.5
            out_hidden[e + q] = jnp.where(live, fresh, state)
            heads = nt(head_w, fresh)
            jac = heads[0:32]
            weighted = jac * jax.nn.softplus(heads[32:64])
            at16 = pl.ds(pl.multiple_of((e + q) * 16, 16), 16)
            jall[at16] = jnp.concatenate([jac[0:16], jac[16:32]], axis=1).astype(BF)
            wall[at16] = jnp.concatenate([weighted[0:16], weighted[16:32]], axis=1).astype(BF)

    grouped(finish)

    same = (iota((128, 128), 0) >> 4) == (iota((128, 128), 1) >> 4)
    square = jnp.where(same, nt(wall[...], jall[...]), 0.0)
    blocks = square[0:16]
    for e in range(1, edges):
        blocks = blocks + square[e * 16 : (e + 1) * 16]
    alive = (iota((16, 128), 1) >> 4) < meta_s[me, 0, 24]
    gpart[...] = jnp.where(alive, blocks * (1.0 / (MAPH * width)), 0.0)

    def tile_copy(rel):
        return remote(
            gpart, gtile.at[tile], s_gt.at[rel], r_gt.at[rel], me, (tile + rel) % n_tile
        )

    for rel in range(1, n_tile):
        tile_copy(rel).start()
    gtile[tile] = gpart[...]
    for rel in range(1, n_tile):
        remote(
            gpart, gtile.at[(tile - rel + n_tile) % n_tile], s_gt.at[rel], r_gt.at[rel],
            me, (tile + rel) % n_tile,
        ).wait_recv()
    total = gtile[0]
    for k in range(1, n_tile):
        total = total + gtile[k]
    gsum[...] = total

    def edge_copy(rel):
        return remote(gsum, gall.at[me], s_ge.at[rel], r_ge.at[rel], (me + rel) % n_edge, tile)

    for rel in range(1, n_edge):
        edge_copy(rel).start()
    gall[me] = total
    for rel in range(1, n_edge):
        remote(
            gsum, gall.at[(me - rel + n_edge) % n_edge], s_ge.at[rel], r_ge.at[rel],
            (me + rel) % n_edge, tile,
        ).wait_recv()

    for rel in range(1, n_edge):
        meta_copy(rel).wait_send()
        edge_copy(rel).wait_send()
        for s in range(slots):
            feat_copy(rel, s).wait_send()
    for rel in range(1, n_tile):
        tile_copy(rel).wait_send()
    each(n_edge * slots, lambda k: sent_pair(txt_up(k), txt_dn(k)))

    def sent(e):
        sent_pair(hid_up(e), hid_dn(e))
        sent_pair(row_up(mext, s_mup, r_mup, e), row_dn(mext, s_mdn, r_mdn, e))
        sent_pair(row_up(rext, s_rup, r_rup, e), row_dn(rext, s_rdn, r_rdn, e))

    each(edges, sent)


def halves(value):
    high = value.astype(BF)
    return high, (value - high.astype(F32)).astype(BF)


def assemble(dims, meta_s, gall, hidden_h, out_hidden, out_cam, out_diag, held, sem):
    n_edge, n_tile, edges, frames, rows, width, slots = dims
    fetch = pltpu.make_async_copy(hidden_h, held, sem.at[0])
    fetch.start()
    me = lax.axis_index("edge")
    tile = lax.axis_index("tile")
    cam_rows, cam_cols = out_cam.shape
    row_id = iota((cam_rows, 128), 0) + tile * cam_rows
    col_id = iota((cam_cols, 128), 0) + me * cam_cols
    same = (iota((128, 128), 0) >> 4) == (iota((128, 128), 1) >> 4)
    lane = iota((1, 128), 1)
    inner = lane & 15
    digit = jnp.where(inner < 6, inner, inner - 6)
    lefts, lows, rights = [], [], []
    for j in range(n_edge):
        spots = jnp.full((1, 128), -1, jnp.int32)
        for e in range(edges):
            source = (j * frames + meta_s[j, 0, 16 + e]) * 6
            target = (meta_s[j, 0, e] * frames + meta_s[j, 0, 8 + e]) * 6
            here = jnp.where(inner < 6, source, target) + digit
            spots = jnp.where(((lane >> 4) == e) & (inner < 12), here, spots)
        mine = (col_id == spots).astype(F32)
        left = jnp.concatenate([(row_id == spots).astype(F32), mine], axis=0).astype(BF)
        stack = jnp.where(same, jnp.concatenate([gall[j]] * 8, axis=0), 0.0)
        picked = nn(
            jnp.concatenate([left, left], axis=1), jnp.concatenate(halves(stack), axis=0)
        )
        high, low = halves(picked)
        lefts.append(high)
        lows.append(low)
        rights.append(mine.astype(BF))
    placed = nt(jnp.concatenate(lefts + lows, axis=1), jnp.concatenate(rights + rights, axis=1))
    fetch.wait()
    store = pltpu.make_async_copy(held, out_hidden, sem.at[1])
    store.start()
    cam = placed[0:cam_rows]
    row_frame = sixth(iota((cam_rows, cam_cols), 0) + tile * cam_rows)
    col_frame = sixth(iota((cam_rows, cam_cols), 1) + me * cam_cols)
    out_cam[...] = jnp.where(row_frame == col_frame, 0.0, cam)
    own = placed[cam_rows:]
    own_row = sixth(iota((cam_cols, cam_cols), 0))
    own_col = sixth(iota((cam_cols, cam_cols), 1))
    own = jnp.where(own_row == own_col, own, 0.0)
    wide_row = iota((cam_cols, 128), 0)
    wide_lane = iota((cam_cols, 128), 1)
    row_in = wide_row.astype(F32) - 6.0 * sixth(wide_row)
    lane_of = sixth(wide_lane)
    lane_in = wide_lane.astype(F32) - 6.0 * lane_of
    gather = (row_in == lane_in).astype(F32).astype(BF)
    high, low = halves(own)
    spread = jnp.where(row_in == lane_of, nn(high, gather) + nn(low, gather), 0.0)
    fold = (
        sixth(iota((frames, cam_cols), 1)) == iota((frames, cam_cols), 0).astype(F32)
    ).astype(F32).astype(BF)
    high, low = halves(spread)
    out_diag[...] = (nn(fold, high) + nn(fold, low))[:, 0:36]
    store.wait()


def per_device(
    features,
    hidden_state,
    edge_source,
    edge_owner,
    edge_target,
    edge_counts,
    corr_weight,
    gate_weight,
    candidate_weight,
    jacobian_weight,
    confidence_weight,
):
    n_edge, n_tile = lax.axis_size("edge"), lax.axis_size("tile")
    edges = hidden_state.shape[0]
    frames, rows, width, chan = features.shape
    slots = max(2, (2 * edges + n_edge - 1) // n_edge)
    band = rows * width
    owners = edge_owner[:, 0]

    fields = ((owners, 0), (edge_target, 8), (edge_source, 16), (edge_counts, 24))
    meta = jnp.zeros((1, 128), jnp.int32)
    for field, at in fields:
        meta = meta + jnp.pad(field, (at, 128 - at - field.shape[0]))[None, :]
    dims = (n_edge, n_tile, edges, frames, rows, width, slots)
    total_slots = n_edge * slots
    text_rows = rows + 2 * RADIUS
    text_rows = text_rows + text_rows % 2
    ext = band + 2 * width
    dma = pltpu.SemaphoreType.DMA
    vmem = pl.BlockSpec(memory_space=pltpu.VMEM)
    hbm = pl.BlockSpec(memory_space=pl.ANY)
    state, gall, meta_all = pl.pallas_call(
        functools.partial(kernel, dims),
        out_shape=(
            jax.ShapeDtypeStruct((edges, band, chan), BF),
            jax.ShapeDtypeStruct((n_edge, 16, 128), F32),
            jax.ShapeDtypeStruct((n_edge, 1, 128), jnp.int32),
        ),
        in_specs=[vmem, hbm, hbm, vmem, hbm, hbm, vmem, vmem],
        out_specs=(vmem, vmem, vmem),
        scratch_shapes=[
            pltpu.VMEM((frames, band, chan), BF),
            pltpu.VMEM((2, 8 * width, chan), BF),
            pltpu.VMEM((edges * 16, 2 * band), BF),
            pltpu.VMEM((edges * 16, 2 * band), BF),
            pltpu.SMEM((n_edge, 1, 128), jnp.int32),
            pltpu.VMEM(((n_edge - 1) * slots, band, chan), BF),
            pltpu.VMEM((total_slots, text_rows * width, chan), BF),
            pltpu.VMEM((edges, band, chan), BF),
            pltpu.VMEM((edges, ext, chan), BF),
            pltpu.VMEM((edges, ext, chan), BF),
            pltpu.VMEM((edges, ext, chan), BF),
            pltpu.VMEM((2, ext, 3 * chan), BF),
            pltpu.VMEM((9 * chan, 2 * chan), BF),
            pltpu.VMEM((9 * chan, 3 * chan), BF),
            pltpu.VMEM((9 * chan, chan), BF),
            pltpu.VMEM((edges, band, 2 * chan), F32),
            pltpu.VMEM((edges, band, chan), F32),
            pltpu.VMEM((edges, band, chan), F32),
            pltpu.VMEM((16, 128), F32),
            pltpu.VMEM((n_tile, 16, 128), F32),
            pltpu.VMEM((16, 128), F32),
            dma((2,)),
            dma((36,)),
            dma((n_edge,)),
            dma((n_edge,)),
            dma,
            dma((total_slots,)),
            dma((total_slots,)),
        ]
        + [dma((total_slots,))] * 4
        + [dma((edges,))] * 12
        + [dma((n_tile,)), dma((n_tile,)), dma((n_edge,)), dma((n_edge,))],
        compiler_params=pltpu.CompilerParams(
            collective_id=0, has_side_effects=True, vmem_limit_bytes=56 * 1024 * 1024
        ),
    )(
        meta,
        features.reshape(frames, band, chan),
        hidden_state.reshape(edges, band, chan),
        corr_weight,
        gate_weight,
        candidate_weight,
        jacobian_weight.T,
        confidence_weight.T,
    )
    hidden_next, cam, diag = pl.pallas_call(
        functools.partial(assemble, dims),
        out_shape=(
            jax.ShapeDtypeStruct((edges, band, chan), BF),
            jax.ShapeDtypeStruct((frames * n_edge * 6 // n_tile, frames * 6), F32),
            jax.ShapeDtypeStruct((frames, 36), F32),
        ),
        in_specs=[pl.BlockSpec(memory_space=pltpu.SMEM), vmem, hbm],
        out_specs=(hbm, vmem, vmem),
        scratch_shapes=[pltpu.VMEM((edges, band, chan), BF), dma((2,))],
    )(meta_all, gall, state)
    return hidden_next.reshape(hidden_state.shape), cam, diag


def solution(mesh):
    placed = (
        P("edge", "tile", None, None),
        P("edge", "tile", None, None),
        P("edge"),
        P("edge", None),
        P("edge"),
        P("edge"),
        P(),
        P(),
        P(),
        P(),
        P(),
    )
    return jax.shard_map(
        per_device,
        mesh=mesh,
        in_specs=placed,
        out_specs=(P("edge", "tile", None, None), P("tile", "edge"), P("edge", None)),
        check_vma=False,
    )
```

```python
import functools

import jax
import jax.numpy as jnp
from jax import lax
from jax.experimental import pallas as pl
from jax.experimental.pallas import tpu as pltpu
from jax.sharding import PartitionSpec as P

MAPH = 48
WINDOW = 7
RADIUS = WINDOW // 2
MESH = pl.DeviceIdType.MESH
HIGH = lax.Precision.HIGHEST
BF = jnp.bfloat16
F32 = jnp.float32


def nt(a, b, precision=None):
    return lax.dot_general(
        a, b, (((1,), (1,)), ((), ())), preferred_element_type=F32, precision=precision
    )


def nn(a, b, precision=None):
    return lax.dot_general(
        a, b, (((1,), (0,)), ((), ())), preferred_element_type=F32, precision=precision
    )


def iota(shape, dim):
    return lax.broadcasted_iota(jnp.int32, shape, dim)


def sixth(index):
    return jnp.floor((index.astype(F32) + 0.5) * (1.0 / 6.0))


def kernel(
    dims,
    meta_in,
    feat_h,
    hidden_h,
    corr_in,
    gate_w,
    cand_w,
    jac_in,
    conf_in,
    out_hidden,
    gall,
    meta_all,
    feat,
    held,
    l_out,
    corr_w,
    jall,
    wall,
    meta_s,
    send,
    text,
    sref,
    hext,
    mext,
    rext,
    x3,
    wh,
    wm,
    wr,
    gpre,
    cpre,
    upd,
    gpart,
    gtile,
    gsum,
    l_in,
    l_w,
    s_meta,
    r_meta,
    l_meta,
    s_feat,
    r_feat,
    s_tup,
    r_tup,
    s_tdn,
    r_tdn,
    s_hup,
    r_hup,
    s_hdn,
    r_hdn,
    s_mup,
    r_mup,
    s_mdn,
    r_mdn,
    s_rup,
    r_rup,
    s_rdn,
    r_rdn,
    s_gt,
    r_gt,
    s_ge,
    r_ge,
):
    n_edge, n_tile, edges, frames, rows, width, slots = dims
    band = rows * width
    halo = RADIUS * width
    me = lax.axis_index("edge")
    tile = lax.axis_index("tile")
    up, down = tile - 1, tile + 1
    has_up, has_down = tile > 0, tile < n_tile - 1

    loads = [
        pltpu.make_async_copy(feat_h, feat, l_in.at[0]),
        pltpu.make_async_copy(hidden_h, hext.at[:, pl.ds(width, band)], l_in.at[1]),
    ]
    fills = []
    for a in range(3):
        for b in range(3):
            at = pl.ds((a * 3 + b) * 128, 128)
            first, second = pl.ds(0, 128), pl.ds(128, 128)
            pairs = (
                (gate_w.at[a, b, first], wh.at[at]),
                (gate_w.at[a, b, second], wm.at[at, pl.ds(0, 256)]),
                (cand_w.at[a, b, second], wm.at[at, pl.ds(256, 128)]),
                (cand_w.at[a, b, first], wr.at[at]),
            )
            for source, target in pairs:
                fills.append(pltpu.make_async_copy(source, target, l_w.at[len(fills)]))
    for load in loads + fills:
        load.start()

    barrier = pltpu.get_barrier_semaphore()
    for rel in range(1, n_edge):
        pl.semaphore_signal(
            barrier, inc=1, device_id=((me + rel) % n_edge, tile), device_id_type=MESH
        )
    for rel in range(1, n_tile):
        pl.semaphore_signal(
            barrier, inc=1, device_id=(me, (tile + rel) % n_tile), device_id_type=MESH
        )
    pl.semaphore_wait(barrier, n_edge + n_tile - 2)

    def remote(src, dst, send_sem, recv_sem, edge_id, tile_id):
        return pltpu.make_async_remote_copy(
            src_ref=src,
            dst_ref=dst,
            send_sem=send_sem,
            recv_sem=recv_sem,
            device_id=(edge_id, tile_id),
            device_id_type=MESH,
        )

    def meta_copy(rel):
        return remote(
            meta_in, meta_all.at[me], s_meta.at[rel], r_meta.at[rel], (me + rel) % n_edge, tile
        )

    for rel in range(1, n_edge):
        meta_copy(rel).start()

    def hid_up(e):
        return remote(
            hidden_h.at[e, pl.ds(0, width)], hext.at[e, pl.ds(width + band, width)],
            s_hup.at[e], r_hup.at[e], me, up,
        )

    def hid_dn(e):
        return remote(
            hidden_h.at[e, pl.ds(band - width, width)], hext.at[e, pl.ds(0, width)],
            s_hdn.at[e], r_hdn.at[e], me, down,
        )

    def row_up(buf, s, r, e):
        return remote(
            buf.at[e, pl.ds(width, width)], buf.at[e, pl.ds(width + band, width)],
            s.at[e], r.at[e], me, up,
        )

    def row_dn(buf, s, r, e):
        return remote(
            buf.at[e, pl.ds(band, width)], buf.at[e, pl.ds(0, width)],
            s.at[e], r.at[e], me, down,
        )

    def txt_up(k):
        return remote(
            text.at[k, pl.ds(halo, halo)], text.at[k, pl.ds(halo + band, halo)],
            s_tup.at[k], r_tup.at[k], me, up,
        )

    def txt_dn(k):
        return remote(
            text.at[k, pl.ds(band, halo)], text.at[k, pl.ds(0, halo)],
            s_tdn.at[k], r_tdn.at[k], me, down,
        )

    def start_pair(make_up, make_dn):
        @pl.when(has_up)
        def _():
            make_up.start()

        @pl.when(has_down)
        def _():
            make_dn.start()

    def recv_pair(make_up, make_dn):
        @pl.when(has_down)
        def _():
            make_up.wait_recv()

        @pl.when(has_up)
        def _():
            make_dn.wait_recv()

    def sent_pair(make_up, make_dn):
        @pl.when(has_up)
        def _():
            make_up.wait_send()

        @pl.when(has_down)
        def _():
            make_dn.wait_send()

    def each(count, body):
        def step(i, carry):
            body(i)
            return carry

        lax.fori_loop(0, count, step, 0)

    each(edges, lambda e: start_pair(hid_up(e), hid_dn(e)))

    zero_row = jnp.zeros((width, 128), BF)
    zero_halo = jnp.zeros((halo, 128), BF)

    @pl.when(tile == 0)
    def _():
        def clear(e):
            for buf in (hext, mext, rext):
                buf[e, pl.ds(0, width)] = zero_row

        each(edges, clear)

        def clear_text(k):
            text[k, pl.ds(0, halo)] = zero_halo

        each(n_edge * slots, clear_text)

    @pl.when(tile == n_tile - 1)
    def _():
        def clear(e):
            for buf in (hext, mext, rext):
                buf[e, pl.ds(width + band, width)] = zero_row

        each(edges, clear)

        def clear_text(k):
            text[k, pl.ds(halo + band, halo)] = zero_halo

        each(n_edge * slots, clear_text)

    if (rows + 2 * RADIUS) % 2:

        def clear_pad(k):
            text[k, pl.ds(band + 2 * halo, width)] = zero_row

        each(n_edge * slots, clear_pad)

    meta_all[me] = meta_in[...]
    for rel in range(1, n_edge):
        remote(
            meta_in, meta_all.at[(me - rel + n_edge) % n_edge], s_meta.at[rel], r_meta.at[rel],
            (me + rel) % n_edge, tile,
        ).wait_recv()
    loads[0].wait()
    local = pltpu.make_async_copy(meta_all, meta_s, l_meta)
    local.start()
    local.wait()

    def asked(peer):
        picks = [jnp.int32(0)] * slots
        rank = jnp.int32(0)
        for k in range(edges):
            hit = (meta_s[peer, 0, k] == me).astype(jnp.int32)
            goal = meta_s[peer, 0, 8 + k]
            for s in range(slots):
                picks[s] = jnp.where((hit == 1) & (rank == s), goal, picks[s])
            rank = rank + hit
        return picks

    def feat_copy(rel, s):
        return remote(
            send.at[(rel - 1) * slots + s],
            text.at[rel * slots + s, pl.ds(halo, band)],
            s_feat.at[rel * slots + s],
            r_feat.at[rel * slots + s],
            (me - rel + n_edge) % n_edge,
            tile,
        )

    asks = [asked((me - rel + n_edge) % n_edge) for rel in range(n_edge)]
    for s in range(slots):
        for rel in range(1, n_edge):
            send[(rel - 1) * slots + s] = feat[asks[rel][s]]
        for rel in range(1, n_edge):
            feat_copy(rel, s).start()
    for s in range(slots):
        text[s, pl.ds(halo, band)] = feat[asks[0][s]]
    for s in range(slots):
        start_pair(txt_up(s), txt_dn(s))

    spot = iota((2 * width, 64), 0)
    rank = ((spot + 97) & 63) - 32
    second = ((spot + 97) & 127) >> 6
    names = iota((2 * width, 64), 1)
    lookup = jnp.concatenate(
        [corr_in[...].astype(F32), jnp.zeros((64 - WINDOW * WINDOW, 128), F32)], axis=0
    ).astype(BF)
    for par in range(2):
        for g in range(4):
            down_by = 2 * g - par + second
            fits = (rank >= -RADIUS) & (rank <= RADIUS) & (down_by >= 0) & (down_by < WINDOW)
            pick = (names == down_by * WINDOW + rank + RADIUS) & fits
            corr_w[par, pl.ds(g * 2 * width, 2 * width)] = nn(
                pick.astype(F32).astype(BF), lookup
            ).astype(BF)

    place12 = iota((32, 64), 0)
    which = place12 >> 4
    within = place12 & 15
    name12 = iota((32, 64), 1)
    pick_j = (within < 12) & (name12 == which * 12 + within)
    padded_jac = jnp.concatenate(
        [jac_in[...].astype(F32), jnp.zeros((40, 128), F32)], axis=0
    ).astype(BF)
    conf_wide = conf_in[...].astype(F32)
    tall = iota((32, 128), 0)
    conf_rows = jnp.where(
        tall < 16,
        jnp.broadcast_to(conf_wide[0:1], (32, 128)),
        jnp.broadcast_to(conf_wide[1:2], (32, 128)),
    )
    head_w = jnp.concatenate(
        [
            nn(pick_j.astype(F32).astype(BF), padded_jac),
            jnp.where((tall & 15) < 12, conf_rows, 0.0),
        ],
        axis=0,
    ).astype(BF)

    col = iota((band + 2 * width, 128), 0) & (width - 1)

    group = 2 if edges % 2 == 0 else 1

    def shifted(buf, first):
        parts = []
        for q in range(group):
            value = buf[first + q]
            wide = value.astype(F32)
            left = jnp.where(col == 0, 0.0, pltpu.roll(wide, 1, 0)).astype(BF)
            right = jnp.where(
                col == width - 1, 0.0, pltpu.roll(wide, band + 2 * width - 1, 0)
            ).astype(BF)
            x3[q, :, 0:128] = left
            x3[q, :, 128:256] = value
            x3[q, :, 256:384] = right
        for q in range(group):
            parts.append(
                jnp.concatenate(
                    [x3[q, a * width : a * width + band] for a in range(3)], axis=1
                )
            )
        return jnp.concatenate(parts, axis=0)

    def grouped(body):
        each(edges // group, lambda i: body(i * group))

    flip_row, flip_col = iota((2 * width, 2 * width), 0), iota((2 * width, 2 * width), 1)
    flip = (
        ((flip_row >= width) == (flip_col >= width))
        & ((flip_row & (width - 1)) + (flip_col & (width - 1)) == width - 1)
    ).astype(F32).astype(BF)

    def flipped(value):
        count = value.shape[0]
        return nn(flip[0:count, 0:count], value).astype(BF)

    def state_part(e):
        for q in range(group):
            recv_pair(hid_up(e + q), hid_dn(e + q))
        for q in range(group):
            source = feat[meta_s[me, 0, 16 + e + q]]
            for first in range(0, rows, 2):
                last = min(rows, first + 2) * width
                sref[e + q, pl.ds(first * width, last - first * width)] = flipped(
                    source[first * width : last]
                )
        value = nn(shifted(hext, e), wh[...])
        for q in range(group):
            gpre[e + q] = value[q * band : (q + 1) * band]

    loads[1].wait()
    for fill in fills:
        fill.wait()
    grouped(state_part)

    for s in range(slots):
        for rel in range(1, n_edge):
            feat_copy(rel, s).wait_recv()
            start_pair(txt_up(rel * slots + s), txt_dn(rel * slots + s))
    each(n_edge * slots, lambda k: recv_pair(txt_up(k), txt_dn(k)))

    lane = iota((width, 128), 1)
    place = (width - 1 - iota((width, 128), 0)) + ((lane + 97) & 63) - 32
    inside = (place >= 0) & (place < width)
    scale = 128.0 ** (-0.5)

    def slot_of(e):
        mine = meta_s[me, 0, e]
        rank = jnp.int32(0)
        for k in range(edges):
            rank = rank + jnp.where((meta_s[me, 0, k] == mine) & (k < e), 1, 0)
        return ((mine - me + n_edge) % n_edge) * slots + jnp.minimum(rank, slots - 1)

    def motion_of(e):
        k = slot_of(e)
        source = sref[e]
        target = text[k]
        for first in range(0, rows, 2):
            count = min(2, rows - first)
            table = nt(
                source[first * width : (first + count) * width],
                target[first * width : (first + 8) * width],
            )
            values = []
            for par in range(count):
                parts = []
                for g in range(4):
                    piece = table[par * width : (par + 1) * width, g * 128 : (g + 1) * 128]
                    moved = pltpu.roll(piece, 0, 1, stride=1, stride_axis=0)
                    parts.append(jnp.where(inside, moved * scale, 0.0).astype(BF))
                value = nn(jnp.concatenate(parts, axis=1), corr_w[par])
                values.append(jnp.maximum(value, 0.0).astype(BF))
            mext[e, pl.ds((first + 1) * width, count * width)] = flipped(
                jnp.concatenate(values, axis=0)
            )

    def motion(e):
        for q in range(group):
            motion_of(e + q)
        for q in range(group):
            start_pair(
                row_up(mext, s_mup, r_mup, e + q), row_dn(mext, s_mdn, r_mdn, e + q)
            )

    grouped(motion)

    def gates(e):
        for q in range(group):
            recv_pair(
                row_up(mext, s_mup, r_mup, e + q), row_dn(mext, s_mdn, r_mdn, e + q)
            )
        both = nn(shifted(mext, e), wm[...])
        for q in range(group):
            part = both[q * band : (q + 1) * band]
            cpre[e + q] = part[:, 256:384]
            gate = jax.nn.sigmoid(gpre[e + q] + part[:, 0:256])
            upd[e + q] = gate[:, 0:128]
            state = hext[e + q, pl.ds(width, band)].astype(F32)
            rext[e + q, pl.ds(width, band)] = (gate[:, 128:256] * state).astype(BF)
        for q in range(group):
            start_pair(
                row_up(rext, s_rup, r_rup, e + q), row_dn(rext, s_rdn, r_rdn, e + q)
            )

    grouped(gates)

    def finish(e):
        for q in range(group):
            recv_pair(
                row_up(rext, s_rup, r_rup, e + q), row_dn(rext, s_rdn, r_rdn, e + q)
            )
        mixed = nn(shifted(rext, e), wr[...])
        for q in range(group):
            candidate = jnp.tanh(cpre[e + q] + mixed[q * band : (q + 1) * band])
            update = upd[e + q]
            state = hext[e + q, pl.ds(width, band)]
            fresh = ((1.0 - update) * state.astype(F32) + update * candidate).astype(BF)
            used = (e + q < meta_s[me, 0, 24]).astype(F32)
            live = jnp.full((band, 128), used) > 0.5
            held[e + q] = jnp.where(live, fresh, state)
            heads = nt(head_w, fresh)
            jac = heads[0:32]
            weighted = jac * jax.nn.softplus(heads[32:64])
            at16 = pl.ds(pl.multiple_of((e + q) * 16, 16), 16)
            jall[at16] = jnp.concatenate([jac[0:16], jac[16:32]], axis=1).astype(BF)
            wall[at16] = jnp.concatenate([weighted[0:16], weighted[16:32]], axis=1).astype(BF)

    grouped(finish)
    store = pltpu.make_async_copy(held, out_hidden, l_out)
    store.start()

    same = (iota((128, 128), 0) >> 4) == (iota((128, 128), 1) >> 4)
    square = jnp.where(same, nt(wall[...], jall[...]), 0.0)
    blocks = square[0:16]
    for e in range(1, edges):
        blocks = blocks + square[e * 16 : (e + 1) * 16]
    alive = (iota((16, 128), 1) >> 4) < meta_s[me, 0, 24]
    gpart[...] = jnp.where(alive, blocks * (1.0 / (MAPH * width)), 0.0)

    def tile_copy(rel):
        return remote(
            gpart, gtile.at[tile], s_gt.at[rel], r_gt.at[rel], me, (tile + rel) % n_tile
        )

    for rel in range(1, n_tile):
        tile_copy(rel).start()
    gtile[tile] = gpart[...]
    for rel in range(1, n_tile):
        remote(
            gpart, gtile.at[(tile - rel + n_tile) % n_tile], s_gt.at[rel], r_gt.at[rel],
            me, (tile + rel) % n_tile,
        ).wait_recv()
    total = gtile[0]
    for k in range(1, n_tile):
        total = total + gtile[k]
    gsum[...] = total

    def edge_copy(rel):
        return remote(gsum, gall.at[me], s_ge.at[rel], r_ge.at[rel], (me + rel) % n_edge, tile)

    for rel in range(1, n_edge):
        edge_copy(rel).start()
    gall[me] = total
    for rel in range(1, n_edge):
        remote(
            gsum, gall.at[(me - rel + n_edge) % n_edge], s_ge.at[rel], r_ge.at[rel],
            (me + rel) % n_edge, tile,
        ).wait_recv()

    store.wait()
    for rel in range(1, n_edge):
        meta_copy(rel).wait_send()
        edge_copy(rel).wait_send()
        for s in range(slots):
            feat_copy(rel, s).wait_send()
    for rel in range(1, n_tile):
        tile_copy(rel).wait_send()
    each(n_edge * slots, lambda k: sent_pair(txt_up(k), txt_dn(k)))

    def sent(e):
        sent_pair(hid_up(e), hid_dn(e))
        sent_pair(row_up(mext, s_mup, r_mup, e), row_dn(mext, s_mdn, r_mdn, e))
        sent_pair(row_up(rext, s_rup, r_rup, e), row_dn(rext, s_rdn, r_rdn, e))

    each(edges, sent)


def halves(value):
    high = value.astype(BF)
    return high, (value - high.astype(F32)).astype(BF)


def assemble(dims, meta_s, gall, hidden_h, out_hidden, out_cam, out_diag, held, sem):
    n_edge, n_tile, edges, frames, rows, width, slots = dims
    fetch = pltpu.make_async_copy(hidden_h, held, sem.at[0])
    fetch.start()
    me = lax.axis_index("edge")
    tile = lax.axis_index("tile")
    cam_rows, cam_cols = out_cam.shape
    row_id = iota((cam_rows, 128), 0) + tile * cam_rows
    col_id = iota((cam_cols, 128), 0) + me * cam_cols
    same = (iota((128, 128), 0) >> 4) == (iota((128, 128), 1) >> 4)
    lane = iota((1, 128), 1)
    inner = lane & 15
    digit = jnp.where(inner < 6, inner, inner - 6)
    lefts, lows, rights = [], [], []
    for j in range(n_edge):
        spots = jnp.full((1, 128), -1, jnp.int32)
        for e in range(edges):
            source = (j * frames + meta_s[j, 0, 16 + e]) * 6
            target = (meta_s[j, 0, e] * frames + meta_s[j, 0, 8 + e]) * 6
            here = jnp.where(inner < 6, source, target) + digit
            spots = jnp.where(((lane >> 4) == e) & (inner < 12), here, spots)
        mine = (col_id == spots).astype(F32)
        left = jnp.concatenate([(row_id == spots).astype(F32), mine], axis=0).astype(BF)
        stack = jnp.where(same, jnp.concatenate([gall[j]] * 8, axis=0), 0.0)
        picked = nn(
            jnp.concatenate([left, left], axis=1), jnp.concatenate(halves(stack), axis=0)
        )
        high, low = halves(picked)
        lefts.append(high)
        lows.append(low)
        rights.append(mine.astype(BF))
    placed = nt(jnp.concatenate(lefts + lows, axis=1), jnp.concatenate(rights + rights, axis=1))
    fetch.wait()
    store = pltpu.make_async_copy(held, out_hidden, sem.at[1])
    store.start()
    cam = placed[0:cam_rows]
    row_frame = sixth(iota((cam_rows, cam_cols), 0) + tile * cam_rows)
    col_frame = sixth(iota((cam_rows, cam_cols), 1) + me * cam_cols)
    out_cam[...] = jnp.where(row_frame == col_frame, 0.0, cam)
    own = placed[cam_rows:]
    own_row = sixth(iota((cam_cols, cam_cols), 0))
    own_col = sixth(iota((cam_cols, cam_cols), 1))
    own = jnp.where(own_row == own_col, own, 0.0)
    wide_row = iota((cam_cols, 128), 0)
    wide_lane = iota((cam_cols, 128), 1)
    row_in = wide_row.astype(F32) - 6.0 * sixth(wide_row)
    lane_of = sixth(wide_lane)
    lane_in = wide_lane.astype(F32) - 6.0 * lane_of
    gather = (row_in == lane_in).astype(F32).astype(BF)
    high, low = halves(own)
    spread = jnp.where(row_in == lane_of, nn(high, gather) + nn(low, gather), 0.0)
    fold = (
        sixth(iota((frames, cam_cols), 1)) == iota((frames, cam_cols), 0).astype(F32)
    ).astype(F32).astype(BF)
    high, low = halves(spread)
    out_diag[...] = (nn(fold, high) + nn(fold, low))[:, 0:36]
    store.wait()


def per_device(
    features,
    hidden_state,
    edge_source,
    edge_owner,
    edge_target,
    edge_counts,
    corr_weight,
    gate_weight,
    candidate_weight,
    jacobian_weight,
    confidence_weight,
):
    n_edge, n_tile = lax.axis_size("edge"), lax.axis_size("tile")
    edges = hidden_state.shape[0]
    frames, rows, width, chan = features.shape
    slots = max(2, (2 * edges + n_edge - 1) // n_edge)
    band = rows * width
    owners = edge_owner[:, 0]

    fields = ((owners, 0), (edge_target, 8), (edge_source, 16), (edge_counts, 24))
    meta = jnp.zeros((1, 128), jnp.int32)
    for field, at in fields:
        meta = meta + jnp.pad(field, (at, 128 - at - field.shape[0]))[None, :]
    dims = (n_edge, n_tile, edges, frames, rows, width, slots)
    total_slots = n_edge * slots
    text_rows = rows + 2 * RADIUS
    text_rows = text_rows + text_rows % 2
    ext = band + 2 * width
    dma = pltpu.SemaphoreType.DMA
    vmem = pl.BlockSpec(memory_space=pltpu.VMEM)
    hbm = pl.BlockSpec(memory_space=pl.ANY)
    state, gall, meta_all = pl.pallas_call(
        functools.partial(kernel, dims),
        out_shape=(
            jax.ShapeDtypeStruct((edges, band, chan), BF),
            jax.ShapeDtypeStruct((n_edge, 16, 128), F32),
            jax.ShapeDtypeStruct((n_edge, 1, 128), jnp.int32),
        ),
        in_specs=[vmem, hbm, hbm, vmem, hbm, hbm, vmem, vmem],
        out_specs=(hbm, vmem, vmem),
        scratch_shapes=[
            pltpu.VMEM((frames, band, chan), BF),
            pltpu.VMEM((edges, band, chan), BF),
            dma,
            pltpu.VMEM((2, 8 * width, chan), BF),
            pltpu.VMEM((edges * 16, 2 * band), BF),
            pltpu.VMEM((edges * 16, 2 * band), BF),
            pltpu.SMEM((n_edge, 1, 128), jnp.int32),
            pltpu.VMEM(((n_edge - 1) * slots, band, chan), BF),
            pltpu.VMEM((total_slots, text_rows * width, chan), BF),
            pltpu.VMEM((edges, band, chan), BF),
            pltpu.VMEM((edges, ext, chan), BF),
            pltpu.VMEM((edges, ext, chan), BF),
            pltpu.VMEM((edges, ext, chan), BF),
            pltpu.VMEM((2, ext, 3 * chan), BF),
            pltpu.VMEM((9 * chan, 2 * chan), BF),
            pltpu.VMEM((9 * chan, 3 * chan), BF),
            pltpu.VMEM((9 * chan, chan), BF),
            pltpu.VMEM((edges, band, 2 * chan), F32),
            pltpu.VMEM((edges, band, chan), F32),
            pltpu.VMEM((edges, band, chan), F32),
            pltpu.VMEM((16, 128), F32),
            pltpu.VMEM((n_tile, 16, 128), F32),
            pltpu.VMEM((16, 128), F32),
            dma((2,)),
            dma((36,)),
            dma((n_edge,)),
            dma((n_edge,)),
            dma,
            dma((total_slots,)),
            dma((total_slots,)),
        ]
        + [dma((total_slots,))] * 4
        + [dma((edges,))] * 12
        + [dma((n_tile,)), dma((n_tile,)), dma((n_edge,)), dma((n_edge,))],
        compiler_params=pltpu.CompilerParams(
            collective_id=0, has_side_effects=True, vmem_limit_bytes=56 * 1024 * 1024
        ),
    )(
        meta,
        features.reshape(frames, band, chan),
        hidden_state.reshape(edges, band, chan),
        corr_weight,
        gate_weight,
        candidate_weight,
        jacobian_weight.T,
        confidence_weight.T,
    )
    hidden_next, cam, diag = pl.pallas_call(
        functools.partial(assemble, dims),
        out_shape=(
            jax.ShapeDtypeStruct((edges, band, chan), BF),
            jax.ShapeDtypeStruct((frames * n_edge * 6 // n_tile, frames * 6), F32),
            jax.ShapeDtypeStruct((frames, 36), F32),
        ),
        in_specs=[pl.BlockSpec(memory_space=pltpu.SMEM), vmem, hbm],
        out_specs=(hbm, vmem, vmem),
        scratch_shapes=[pltpu.VMEM((edges, band, chan), BF), dma((2,))],
    )(meta_all, gall, state)
    return hidden_next.reshape(hidden_state.shape), cam, diag


def solution(mesh):
    placed = (
        P("edge", "tile", None, None),
        P("edge", "tile", None, None),
        P("edge"),
        P("edge", None),
        P("edge"),
        P("edge"),
        P(),
        P(),
        P(),
        P(),
        P(),
    )
    return jax.shard_map(
        per_device,
        mesh=mesh,
        in_specs=placed,
        out_specs=(P("edge", "tile", None, None), P("tile", "edge"), P("edge", None)),
        check_vma=False,
    )
```
